32 devices in a mesh: dp: 2 (over core), ctx: 4 (over y, x), tp: 4 (over z).
Axes of the slice: x: 2, y: 2, z: 4, core: 2. Of those that a mesh axis runs over, the one named last changes fastest.
Arguments:
- layer_input: bfloat16 [6, 1024, 2048], P('dp', 'ctx'), may hold values from -6 to 6
- segments: int32 [6, 1024], P('dp', 'ctx'), may hold values from 0 to 3, never falling along the last dimension, each value on 1 to 384 neighbouring positions
- cotangent: bfloat16 [6, 1024, 2048], P('dp', 'ctx'), may hold values from -6 to 6
- norm1_gain: float32 [2048], replicated, may hold values from 0.5 to 1.5
- norm2_gain: float32 [2048], replicated, may hold values from 0.5 to 1.5
- head_gain: float32 [512], replicated, may hold values from 0.5 to 1.5
- decay_bias: float32 [256], replicated, may hold values from 0 to 10
- w_query: bfloat16 [2048, 2048], P(('dp', 'ctx'), 'tp'), may hold values from -0.375 to 0.375
- w_key: bfloat16 [2048, 2048], P(('dp', 'ctx'), 'tp'), may hold values from -0.375 to 0.375
- w_value: bfloat16 [2048, 2048], P(('dp', 'ctx'), 'tp'), may hold values from -0.125 to 0.125
- w_decay: bfloat16 [2048, 256], P(('dp', 'ctx'), 'tp'), may hold values from -0.125 to 0.125
- w_out: bfloat16 [2048, 2048], P('tp', ('dp', 'ctx')), may hold values from -0.125 to 0.125
- w_gate: bfloat16 [2048, 5632], P(('dp', 'ctx'), 'tp'), may hold values from -0.125 to 0.125
- w_up: bfloat16 [2048, 5632], P(('dp', 'ctx'), 'tp'), may hold values from -0.125 to 0.125
- w_down: bfloat16 [5632, 2048], P('tp', ('dp', 'ctx')), may hold values from -0.078125 to 0.078125
Outputs:
- output: bfloat16 [6, 1024, 2048], P('dp', 'ctx')
- input_grad: float32 [6, 1024, 2048], P('dp', 'ctx')
- norm1_gain_grad: float32 [2048], replicated
- norm2_gain_grad: float32 [2048], replicated
- head_gain_grad: float32 [512], replicated
- decay_bias_grad: float32 [256], replicated
- w_query_grad: float32 [2048, 2048], P(('dp', 'ctx'), 'tp')
- w_key_grad: float32 [2048, 2048], P(('dp', 'ctx'), 'tp')
- w_value_grad: float32 [2048, 2048], P(('dp', 'ctx'), 'tp')
- w_decay_grad: float32 [2048, 256], P(('dp', 'ctx'), 'tp')
- w_out_grad: float32 [2048, 2048], P('tp', ('dp', 'ctx'))
- w_gate_grad: float32 [2048, 5632], P(('dp', 'ctx'), 'tp')
- w_up_grad: float32 [2048, 5632], P(('dp', 'ctx'), 'tp')
- w_down_grad: float32 [5632, 2048], P('tp', ('dp', 'ctx'))
The draws below stay inside these ranges and needn't reach their ends.
Inputs may be any that keep to these rules, and one draw needn't show every extreme that they name: `segments`: within each sequence the numbers never fall, start at 0 and take every value up to 3; a document holds 1 to 384 tokens, and some document holds exactly 384.
All inputs are finite; a program needn't handle non-finite values.
Results may differ from the reference program's by a relative error of at most 0.012.
The reference program's roundings to bfloat16 on the way count: a program that leaves them out, or rounds other values in their place, can miss the bound.
Values may be sent and summed in bfloat16 or wider, within the bound.
No kernel may reach another device: no remote copies, remote signals or barrier semaphores. Data moves between devices by JAX's collectives and lax.ppermute only.
A program may use at most 256 MiB of HBM per device.

```python
import math
import jax
import jax.numpy as jnp
import numpy as np
from jax import lax

D = 2048
HEADS = 4
HEAD_DIM = 512
SLOTS = 64
FF = 5632
TOK_DEV = 256
LEN = 1024
SEQS = 6
DOCS = 4
DOC_MOST = 384


def level_of(key, extent, pieces, low, high):
    factor_of, own = 1.0, jax.random.fold_in(key, 6)
    for dim, blocks in pieces:
        steps = jnp.exp(jax.random.uniform(jax.random.fold_in(own, dim), (blocks,), jnp.float32, low / len(pieces), high / len(pieces)))
        factor_of = factor_of * jnp.repeat(steps, extent[dim] // blocks).reshape([-1 if axis == dim else 1 for axis in range(len(extent))])
    return factor_of


def split_up(count, total, bound, slope):
    weights = [(1 << 20) // math.isqrt(rank ** slope) + 1 for rank in range(2, count + 1)]
    rest, given = total - bound - (count - 1), [1] * (count - 1)
    while rest > 0:
        movable = [i for i in range(count - 1) if given[i] < bound]
        mass, remaining = sum([weights[i] for i in movable]), rest
        for i in movable:
            addition = min(bound - given[i], max(1, remaining * weights[i] // mass), rest)
            given[i] = given[i] + addition
            rest = rest - addition
    return np.array([bound] + given)


def ragged_sizes(rng, amount, total, limit, skew):
    if amount == 2:
        one = jax.random.randint(rng, (), max(1, total - limit), min(limit, total - 1) + 1)
        return jnp.stack([one, total - one])
    tallies = jnp.asarray(split_up(amount, total, limit, skew), jnp.int32)
    twos = (amount - 1) // 2
    donor, receiver = tallies[1:1 + 2 * twos:2], tallies[2:2 + 2 * twos:2]
    room = jnp.minimum(donor - 1, limit - receiver)
    shifted = jax.random.randint(jax.random.fold_in(rng, 1), (twos,), 0, 1 << 20) % (room + 1)
    tallies = tallies.at[1:1 + 2 * twos:2].set(donor - shifted).at[2:2 + 2 * twos:2].set(receiver + shifted)
    return tallies[jax.random.permutation(jax.random.fold_in(rng, 2), amount)]


def centred(rng, shape, width, most, cuts=(), kind=jnp.bfloat16):
    values = width * jax.random.normal(rng, shape, jnp.float32)
    if cuts:
        values = values * level_of(rng, shape, cuts, -0.22, 0.18)
    return jnp.clip(values, -most, most).astype(kind)


def setup_inputs(seed: int = 0) -> dict:
    key_list = jax.random.split(jax.random.key(seed), 16)
    return {
        "layer_input": centred(key_list[0], (SEQS, LEN, D), 1.0, 6.0, ((0, 2), (1, 4))),
        "segments": jax.vmap(lambda own: jnp.searchsorted(jnp.cumsum(ragged_sizes(own, DOCS, LEN, DOC_MOST, 2)), jnp.arange(LEN), side="right"))(jax.random.split(key_list[1], SEQS)).reshape((SEQS, LEN)).astype(jnp.int32),
        "cotangent": centred(key_list[2], (SEQS, LEN, D), 1.0, 6.0, ((0, 2), (1, 4))),
        "norm1_gain": jnp.clip(1.0 + 0.1 * jax.random.normal(key_list[3], (D,), jnp.float32), 0.5, 1.5),
        "norm2_gain": jnp.clip(1.0 + 0.1 * jax.random.normal(key_list[4], (D,), jnp.float32), 0.5, 1.5),
        "head_gain": jnp.clip(1.0 + 0.1 * jax.random.normal(key_list[5], (HEAD_DIM,), jnp.float32), 0.5, 1.5),
        "decay_bias": jnp.clip(jax.random.uniform(key_list[6], (HEADS * SLOTS,), jnp.float32, 0.0, 10.0), 0.0, 10.0),
        "w_query": centred(key_list[7], (D, HEADS * HEAD_DIM), (D // 8) ** -0.5, 0.375, ((0, 8), (1, 4))),
        "w_key": centred(key_list[8], (D, HEADS * HEAD_DIM), (D // 8) ** -0.5, 0.375, ((0, 8), (1, 4))),
        "w_value": centred(key_list[9], (D, HEADS * HEAD_DIM), D ** -0.5, 0.125, ((0, 8), (1, 4))),
        "w_decay": centred(key_list[10], (D, HEADS * SLOTS), D ** -0.5, 0.125, ((0, 8), (1, 4))),
        "w_out": centred(key_list[11], (HEADS * HEAD_DIM, D), (HEADS * HEAD_DIM) ** -0.5, 0.125, ((0, 4), (1, 8))),
        "w_gate": centred(key_list[12], (D, FF), D ** -0.5, 0.125, ((0, 8), (1, 4))),
        "w_up": centred(key_list[13], (D, FF), D ** -0.5, 0.125, ((0, 8), (1, 4))),
        "w_down": centred(key_list[14], (FF, D), FF ** -0.5, 0.078125, ((0, 4), (1, 8))),
    }


epsilon = 1e-05
gate_norm = 8.0
highest = lax.Precision.HIGHEST

@jax.custom_vjp
def low(v):
    return lax.optimization_barrier(v.astype(jnp.bfloat16)).astype(jnp.float32)

@jax.custom_vjp
def low_back(v):
    return v

def low_keep(v):
    return (low(v), None)

def low_pass(kept, grad):
    return (grad,)

def back_keep(v):
    return (v, None)

def back_low(kept, grad):
    return (low(grad),)
low.defvjp(low_keep, low_pass)
low_back.defvjp(back_keep, back_low)

def matmul(left, right):
    return jnp.dot(left, right, precision=highest, preferred_element_type=jnp.float32)

def rms_scale(array, gain_vec):
    factor = lax.rsqrt(lax.optimization_barrier(jnp.mean(array * array, axis=-1, keepdims=True)) + epsilon)
    return array * factor * gain_vec

def decay_terms(log_decay, seg_ids):
    count = log_decay.shape[0]
    levels = jnp.cumsum(log_decay, axis=0)
    position = jnp.arange(count)
    same_doc = (seg_ids[:, None] == seg_ids[None, :]) & (position[:, None] >= position[None, :])
    spread = jnp.where(same_doc[:, :, None], levels[:, None, :] - levels[None, :, :], -jnp.inf)
    weights = jnp.exp(spread) * (-jnp.expm1(log_decay))[None, :, :]
    carried = jnp.exp(levels) * (seg_ids == seg_ids[0]).astype(jnp.float32)[:, None]
    return (weights, carried)

def slot_full(queries, key_rows, values_all, log_decay, seg_ids, key_in, value_in):
    weights, carried = decay_terms(log_decay, seg_ids)
    qk_dots = matmul(queries, key_rows.T)
    scores = jnp.einsum('tsm,ts->tm', weights, qk_dots, precision=highest) + carried * matmul(queries, key_in.T)
    slot_probs = jax.nn.softmax(scores * HEAD_DIM ** (-0.5), axis=-1)
    mixing = jnp.einsum('tsm,tm->ts', weights, slot_probs, precision=highest)
    return matmul(mixing, values_all) + matmul(slot_probs * carried, value_in)

def slot_final(key_rows, values_all, log_decay, seg_ids, key_in, value_in):
    levels = jnp.cumsum(log_decay, axis=0)
    tail_weights = jnp.exp(levels[-1][None, :] - levels) * -jnp.expm1(log_decay) * (seg_ids == seg_ids[-1]).astype(jnp.float32)[:, None]
    decay_end = jnp.exp(levels[-1]) * (seg_ids[-1] == seg_ids[0]).astype(jnp.float32)
    return (decay_end[:, None] * key_in + matmul(tail_weights.T, key_rows), decay_end[:, None] * value_in + matmul(tail_weights.T, values_all))

def block_step(carried_state, block_in):
    key_state, value_state, last_doc = carried_state
    queries, key_rows, values_all, log_decay, seg_ids = block_in
    linked = (last_doc == seg_ids[0].astype(jnp.float32)).astype(jnp.float32)
    key_in = linked * key_state
    value_in = linked * value_state
    block_outs = jax.vmap(slot_full, in_axes=(0, 0, 0, 0, None, 0, 0))(queries, key_rows, values_all, log_decay, seg_ids, key_in, value_in)
    key_next, value_next = jax.vmap(slot_final, in_axes=(0, 0, 0, None, 0, 0))(key_rows, values_all, log_decay, seg_ids, key_in, value_in)
    return ((key_next, value_next, seg_ids[-1].astype(jnp.float32)), block_outs)

def sequence(params, tokens_in, seg_ids):
    gain_one, gain_two, gain_head, bias_all, w_query, w_key, w_value, w_decay, w_out, w_gate, w_up, w_down = params
    length = tokens_in.shape[0]
    normed1 = low(rms_scale(tokens_in, gain_one))

    def head_proj(weight_mat):
        return low_back(low(matmul(normed1, weight_mat))).reshape(length, HEADS, HEAD_DIM).transpose(1, 0, 2)
    queries = head_proj(w_query)
    key_rows = head_proj(w_key)
    values_all = head_proj(w_value)
    logits = low_back(matmul(normed1, w_decay) + bias_all)
    log_decay = (jax.nn.log_sigmoid(logits) / gate_norm).reshape(length, HEADS, SLOTS).transpose(1, 0, 2)
    blocks = length // TOK_DEV

    def to_blocks(array):
        return array.reshape(HEADS, blocks, TOK_DEV, array.shape[-1]).transpose(1, 0, 2, 3)
    start_state = (jnp.zeros((HEADS, SLOTS, HEAD_DIM), jnp.float32), jnp.zeros((HEADS, SLOTS, HEAD_DIM), jnp.float32), jnp.float32(-1.0))
    _, block_outs = lax.scan(jax.checkpoint(block_step), start_state, (to_blocks(queries), to_blocks(key_rows), to_blocks(values_all), to_blocks(log_decay), seg_ids.reshape(blocks, TOK_DEV)))
    mixed_out = block_outs.transpose(1, 0, 2, 3).reshape(HEADS, length, HEAD_DIM)
    normed_o = low(rms_scale(mixed_out, gain_head)).transpose(1, 0, 2).reshape(length, HEADS * HEAD_DIM)
    hidden = tokens_in + low_back(matmul(normed_o, w_out))
    normed2 = low(rms_scale(hidden, gain_two))
    gate_pre = low_back(matmul(normed2, w_gate))
    up_pre = low_back(matmul(normed2, w_up))
    hidden_act = low(jax.nn.silu(gate_pre) * up_pre)
    return hidden + low_back(matmul(hidden_act, w_down))

def reference(layer_input, segments, cotangent, norm1_gain, norm2_gain, head_gain, decay_bias, w_query, w_key, w_value, w_decay, w_out, w_gate, w_up, w_down):
    params = tuple((array.astype(jnp.float32) for array in (norm1_gain, norm2_gain, head_gain, decay_bias, w_query, w_key, w_value, w_decay, w_out, w_gate, w_up, w_down)))
    seq_fn = jax.checkpoint(sequence)

    def forward(param_set, inputs):
        return lax.map(lambda pair_in: seq_fn(param_set, pair_in[0], pair_in[1]), (inputs, segments))
    output, pullback = jax.vjp(forward, params, layer_input.astype(jnp.float32))
    grads, input_grad = pullback(cotangent.astype(jnp.float32))
    return (output.astype(jnp.bfloat16), input_grad, grads[0], grads[1], grads[2], grads[3], grads[4], grads[5], grads[6], grads[7], grads[8], grads[9], grads[10], grads[11])
```

```python
import jax
import jax.numpy as jnp
from jax import lax
from jax.experimental import pallas as pl
from jax.experimental.pallas import tpu as pltpu
from jax.sharding import PartitionSpec as P

HEAD_DIM = 512
SLOTS = 64
CHUNK = 32
epsilon = 1e-05
gate_norm = 8.0
f32 = jnp.float32
bf16 = jnp.bfloat16
NEG = -1e30
SCALE = HEAD_DIM**-0.5


def split2(x):
    high = x.astype(bf16)
    return high, (x - high.astype(f32)).astype(bf16)


def dg(a, b, ca, cb):
    return lax.dot_general(a, b, (((ca,), (cb,)), ((), ())), preferred_element_type=f32)


def dot2(a, b, ca, cb):
    high, low = a
    return dg(high, b, ca, cb) + dg(low, b, ca, cb)


def dot2r(a, b, ca, cb):
    high, low = b
    return dg(a, high, ca, cb) + dg(a, low, ca, cb)


def dot3(a, b, ca, cb):
    return dg(a[0], b[0], ca, cb) + (dg(a[0], b[1], ca, cb) + dg(a[1], b[0], ca, cb))


def group_lane(x, index):
    rows, lanes = x.shape
    lane = lax.broadcasted_iota(jnp.int32, (rows, 128), 1)
    at = (lane // CHUNK) * CHUNK + index
    parts = [
        jnp.take_along_axis(x[:, i : i + 128], at, axis=1, mode="promise_in_bounds")
        for i in range(0, lanes, 128)
    ]
    return jnp.concatenate(parts, axis=1)


def chunk_of(rows, lanes):
    return lax.broadcasted_iota(jnp.int32, (rows, lanes), 1) // CHUNK


def pick_rows(array, rows, chunks, first=0):
    lanes = array.shape[1]
    chunk = chunk_of(rows, lanes)
    total = jnp.zeros((rows, lanes), f32)
    for c in range(first, chunks):
        total = jnp.where(chunk == c, array[(c - first) * rows : (c - first + 1) * rows], total)
    return total


def level_refs(levels):
    slots, tokens = levels.shape
    chunk = chunk_of(slots, tokens)
    refs = jnp.zeros_like(levels)
    for c in range(1, tokens // CHUNK):
        refs = jnp.where(chunk == c, levels[:, c * CHUNK - 1 : c * CHUNK], refs)
    return refs


def stack_chunks(array, chunks):
    chunk = chunk_of(*array.shape)
    return jnp.concatenate([jnp.where(chunk == c, array, 0.0) for c in range(1, chunks)], axis=0)


def aux_rows(tokens):
    chunks = tokens // CHUNK
    base = 2 * CHUNK + chunks
    return base, base + 8


def make_aux(seg, prev_doc):
    count, tokens = seg.shape
    chunks = tokens // CHUNK
    place = jnp.arange(tokens)
    local = place % CHUNK
    grouped = seg.reshape(count, chunks, CHUNK)
    spread = jnp.repeat(grouped.transpose(0, 2, 1), CHUNK, axis=2)
    index = jnp.arange(CHUNK)[:, None]
    same = spread == seg[:, None, :]
    from_j = same & (local[None, :] >= index)[None]
    to_i = same & (local[None, :] <= index)[None]
    ends = jnp.concatenate([jnp.full((count, 1), -5, seg.dtype), grouped[:, :-1, -1]], axis=1)
    before = (ends[:, :, None] == seg[:, None, :]) & (
        place[None, :] < (jnp.arange(chunks) * CHUNK)[:, None]
    )[None]
    after = jnp.repeat(ends, CHUNK, axis=1) == seg
    first = seg == seg[:, :1]
    last = seg == seg[:, -1:]
    bias = jnp.concatenate(
        [from_j, to_i, before, after[:, None], first[:, None], last[:, None]], axis=1
    )
    bias = jnp.where(bias, 0.0, NEG).astype(f32)
    previous = jnp.concatenate([prev_doc[:, None], seg[:, :-1]], axis=1)
    keeps = (previous == seg).astype(f32)[:, None]
    pad = jnp.zeros((count, 4, tokens), f32)
    return jnp.concatenate([bias, keeps, pad], axis=1)


def state_kernel(k_ref, v_ref, ld_ref, one_ref, aux_ref, lev_ref, ks_ref, vs_ref):
    tokens = ld_ref.shape[1]
    base, _ = aux_rows(tokens)
    earlier = lax.broadcasted_iota(jnp.int32, (tokens, tokens), 0)
    later = lax.broadcasted_iota(jnp.int32, (tokens, tokens), 1)
    upper = jnp.where(earlier <= later, 1.0, 0.0).astype(bf16)
    ld = ld_ref[...]
    high, rest = ld.astype(bf16), None
    rest = ld - high.astype(f32)
    mid, low = split2(rest)
    levels = dg(high, upper, 1, 0) + (dg(mid, upper, 1, 0) + dg(low, upper, 1, 0))
    lev_ref[...] = levels
    tail = jnp.exp(levels[:, tokens - 1 : tokens] - levels + aux_ref[0, base + 2 : base + 3, :])
    tail = split2(tail * one_ref[...])
    ks_ref[0] = dot2(tail, k_ref[...], 1, 0)
    vs_ref[0] = dot2(tail, v_ref[...], 1, 0)


def forward_kernel(
    q_ref, k_ref, v_ref, lev_ref, one_ref, aux_ref, ki_ref, vi_ref, gain_ref,
    no_ref, mix_ref, p_ref, sc_ref, mt_ref, w_scr, d_scr, wh_scr, wl_scr,
):
    tokens = lev_ref.shape[1]
    chunks = tokens // CHUNK
    base, _ = aux_rows(tokens)
    levels, one = lev_ref[...], one_ref[...]
    q, k, v = q_ref[...], k_ref[...], v_ref[...]
    chunk = chunk_of(SLOTS, tokens)
    kq = dg(k, q, 1, 1)
    d_scr[...] = pick_rows(kq, CHUNK, chunks)

    def inside(j, scores):
        gap = levels - group_lane(levels, j) + aux_ref[0, pl.ds(j, 1), :]
        w = jnp.exp(gap) * group_lane(one, j)
        w_scr[j] = w
        return scores + w * d_scr[pl.ds(j, 1), :]

    scores = lax.fori_loop(0, CHUNK, inside, jnp.zeros_like(levels), unroll=2)
    decay = jnp.exp(levels - level_refs(levels) + aux_ref[0, base : base + 1, :])
    for c in range(1, chunks):
        w = levels[:, c * CHUNK - 1 : c * CHUNK] - levels + aux_ref[0, 2 * CHUNK + c : 2 * CHUNK + c + 1, :]
        wh, wl = split2(jnp.exp(w) * one)
        wh_scr[(c - 1) * SLOTS : c * SLOTS] = wh
        wl_scr[(c - 1) * SLOTS : c * SLOTS] = wl
    wst = (wh_scr[...], wl_scr[...])
    scores += decay * pick_rows(dot3(wst, split2(kq), 1, 0), SLOTS, chunks, 1)
    carried = jnp.exp(levels + aux_ref[0, base + 1 : base + 2, :])
    scores += carried * dot2(split2(ki_ref[0]), q, 1, 1)
    sc_ref[...] = scores
    z = scores * SCALE
    e = jnp.exp(z - jnp.max(z, axis=0, keepdims=True))
    probs = e / jnp.sum(e, axis=0, keepdims=True)
    p_ref[...] = probs

    def mixing(j, carry):
        d_scr[pl.ds(j, 1), :] = jnp.sum(w_scr[j] * probs, axis=0, keepdims=True)
        return carry

    lax.fori_loop(0, CHUNK, mixing, 0, unroll=2)
    row = lax.broadcasted_iota(jnp.int32, (tokens, tokens), 0) // CHUNK
    col = lax.broadcasted_iota(jnp.int32, (tokens, tokens), 1) // CHUNK
    mixed_t = jnp.where(row == col, jnp.concatenate([d_scr[...]] * chunks, axis=0), 0.0)
    mixed_t += dot3(wst, split2(stack_chunks(probs * decay, chunks)), 0, 0)
    mt_ref[0] = mixed_t
    out = dot2(split2(mixed_t), v, 0, 0) + dot3(split2(probs * carried), split2(vi_ref[0]), 0, 0)
    mix_ref[...] = out
    unit = out * lax.rsqrt(jnp.mean(out * out, axis=1, keepdims=True) + epsilon)
    no_ref[...] = (unit * gain_ref[...]).astype(bf16)


def backward_kernel(
    q_ref, k_ref, v_ref, lev_ref, one_ref, aux_ref, ki_ref, vi_ref, gain_ref, mix_ref, p_ref, sc_ref, mt_ref, go_ref,
    gq_ref, gk_ref, gv_ref, r_ref, a_ref, dk_ref, dv_ref, hg_ref, w_scr, d_scr, e_scr, x_scr, wh_scr, wl_scr,
):
    tokens = lev_ref.shape[1]
    chunks = tokens // CHUNK
    base, _ = aux_rows(tokens)
    levels, one, probs = lev_ref[...], one_ref[...], p_ref[...]
    q, k, v = q_ref[...], k_ref[...], v_ref[...]
    out, go = mix_ref[...], go_ref[...]
    factor = lax.rsqrt(jnp.mean(out * out, axis=1, keepdims=True) + epsilon)
    unit = out * factor
    hg_ref[0] = jnp.sum(go * unit, axis=0, keepdims=True)
    go = go * gain_ref[...]
    grad = factor * (go - unit * jnp.mean(go * unit, axis=1, keepdims=True))
    g = split2(grad)
    kin, vin = split2(ki_ref[0]), split2(vi_ref[0])
    gv = dot2r(v, g, 1, 1)
    d_scr[...] = pick_rows(gv, CHUNK, chunks)

    def inside(j, dp):
        gap = levels - group_lane(levels, j) + aux_ref[0, pl.ds(j, 1), :]
        w = jnp.exp(gap) * group_lane(one, j)
        w_scr[j] = w
        return dp + w * d_scr[pl.ds(j, 1), :]

    dp = lax.fori_loop(0, CHUNK, inside, jnp.zeros_like(levels), unroll=2)
    decay = jnp.exp(levels - level_refs(levels) + aux_ref[0, base : base + 1, :])
    for c in range(1, chunks):
        w = levels[:, c * CHUNK - 1 : c * CHUNK] - levels + aux_ref[0, 2 * CHUNK + c : 2 * CHUNK + c + 1, :]
        w = jnp.exp(w)
        x_scr[(c - 1) * SLOTS : c * SLOTS] = w
        wh, wl = split2(w * one)
        wh_scr[(c - 1) * SLOTS : c * SLOTS] = wh
        wl_scr[(c - 1) * SLOTS : c * SLOTS] = wl
    wst = (wh_scr[...], wl_scr[...])
    dp += decay * pick_rows(dot3(wst, split2(gv), 1, 0), SLOTS, chunks, 1)
    carried = jnp.exp(levels + aux_ref[0, base + 1 : base + 2, :])
    dp += carried * dot3(vin, g, 1, 1)
    dz = SCALE * probs * (dp - jnp.sum(probs * dp, axis=0, keepdims=True))
    a_ref[...] = dz * sc_ref[...] + probs * dp

    def mixing(j, carry):
        d_scr[pl.ds(j, 1), :] = jnp.sum(w_scr[j] * dz, axis=0, keepdims=True)
        return carry

    lax.fori_loop(0, CHUNK, mixing, 0, unroll=2)
    row = lax.broadcasted_iota(jnp.int32, (tokens, tokens), 0) // CHUNK
    col = lax.broadcasted_iota(jnp.int32, (tokens, tokens), 1) // CHUNK
    mz_t = jnp.where(row == col, jnp.concatenate([d_scr[...]] * chunks, axis=0), 0.0)
    zst = split2(stack_chunks(dz * decay, chunks))
    pst = split2(stack_chunks(probs * decay, chunks))
    mz_t += dot3(wst, zst, 0, 0)
    mz = split2(mz_t)
    zc, pc = split2(dz * carried), split2(probs * carried)
    gq_ref[...] = (dot2(mz, k, 0, 0) + dot3(zc, kin, 0, 0)).astype(bf16)
    gk_ref[...] = dot2(mz, q, 1, 0)
    gv_ref[...] = dot3(split2(mt_ref[0]), g, 1, 0)
    dk_ref[0] = dot2(zc, q, 1, 0)
    dv_ref[0] = dot3(pc, g, 1, 0)
    qk = dg(q, k, 1, 1)
    gv_n = dot2(g, v, 1, 1)
    d_scr[...] = pick_rows(qk, CHUNK, chunks)
    e_scr[...] = pick_rows(gv_n, CHUNK, chunks)

    def onward(i, total):
        gap = group_lane(levels, i) - levels + aux_ref[0, pl.ds(CHUNK + i, 1), :]
        term = group_lane(dz, i) * d_scr[pl.ds(i, 1), :] + group_lane(probs, i) * e_scr[pl.ds(i, 1), :]
        return total + jnp.exp(gap) * term

    total = lax.fori_loop(0, CHUNK, onward, jnp.zeros_like(levels), unroll=2)
    cross = dot3(zst, split2(qk), 1, 0) + dot3(pst, split2(gv_n), 1, 0)
    for c in range(1, chunks):
        total += x_scr[(c - 1) * SLOTS : c * SLOTS] * cross[(c - 1) * SLOTS : c * SLOTS]
    r_ref[...] = total


def finish_kernel(
    k_ref, v_ref, lev_ref, one_ref, sig_ref, aux_ref, sums_ref, ki_ref, vi_ref, ks_ref, vs_ref, gk_ref, gv_ref,
    r_ref, a_ref, dk_ref, dv_ref, gko_ref, gvo_ref, gl_ref,
):
    tokens = lev_ref.shape[1]
    base, _ = aux_rows(tokens)
    levels, one = lev_ref[...], one_ref[...]
    k, v = k_ref[...], v_ref[...]
    tail = jnp.exp(levels[:, tokens - 1 : tokens] - levels + aux_ref[0, base + 2 : base + 3, :])
    end = jnp.exp(levels[:, tokens - 1 : tokens] + aux_ref[0, base + 1 : base + 2, tokens - 1 : tokens])
    dk, dv = dk_ref[0], dv_ref[0]
    dks, dvs = split2(dk), split2(dv)
    weights = split2(tail * one)
    gko_ref[...] = (gk_ref[...] + dot3(weights, dks, 0, 0)).astype(bf16)
    gvo_ref[...] = (gv_ref[...] + dot3(weights, dvs, 0, 0)).astype(bf16)
    rows = r_ref[...] + tail * (dot2(dks, k, 1, 1) + dot2(dvs, v, 1, 1))
    final_k = end * ki_ref[0] + ks_ref[0]
    final_v = end * vi_ref[0] + vs_ref[0]
    at_end = jnp.sum(dk * final_k + dv * final_v, axis=1, keepdims=True)
    x = a_ref[...] - one * rows
    high = x.astype(bf16)
    mid, low = split2(x - high.astype(f32))
    sums = sums_ref[0]
    flow = dg(high, sums, 1, 0) + (dg(mid, sums, 1, 0) + dg(low, sums, 1, 0))
    flow += jnp.where(aux_ref[0, base + 2 : base + 3, :] == 0.0, at_end, 0.0)
    grad = flow * aux_ref[0, base + 3 : base + 4, :] - (1.0 - one) * rows
    gl_ref[...] = (grad * sig_ref[...]).astype(bf16)


def seq_specs(tokens):
    def tok(col, width=HEAD_DIM):
        return pl.BlockSpec((tokens, width), lambda i: (i, col))

    lane = pl.BlockSpec((SLOTS, tokens), lambda i: (0, i))
    _, rows = aux_rows(tokens)
    aux = pl.BlockSpec((1, rows, tokens), lambda i: (i, 0, 0))
    state = pl.BlockSpec((1, SLOTS, HEAD_DIM), lambda i: (i, 0, 0))
    gain = pl.BlockSpec((1, HEAD_DIM), lambda i: (0, 0))
    square = pl.BlockSpec((1, tokens, tokens), lambda i: (i, 0, 0))
    row = pl.BlockSpec((1, 1, HEAD_DIM), lambda i: (i, 0, 0))
    return tok, lane, aux, state, gain, square, row


def params(mib):
    return pltpu.CompilerParams(vmem_limit_bytes=mib << 20)


def cost(count, flops, size):
    return pl.CostEstimate(flops=count * flops, bytes_accessed=count * size, transcendentals=count * 1000000)


def shape(dims, dtype):
    return jax.ShapeDtypeStruct(dims, dtype)


def run_states(qkv, ld, one, aux):
    count, _, tokens = aux.shape
    tok, lane, auxs, state, _, _, _ = seq_specs(tokens)
    return pl.pallas_call(
        state_kernel,
        grid=(count,),
        in_specs=[tok(1), tok(2), lane, lane, auxs],
        out_specs=[lane, state, state],
        out_shape=[
            shape((SLOTS, count * tokens), f32),
            shape((count, SLOTS, HEAD_DIM), f32),
            shape((count, SLOTS, HEAD_DIM), f32),
        ],
        compiler_params=params(24),
        cost_estimate=cost(count, 100000000, 1500000),
    )(qkv, qkv, ld, one, aux)


def big_scratch(tokens):
    stack = (tokens // CHUNK - 1) * SLOTS
    return stack


def run_forward(qkv, levels, one, aux, key_in, value_in, gain):
    count, _, tokens = aux.shape
    tok, lane, auxs, state, gains, square, _ = seq_specs(tokens)
    stack = big_scratch(tokens)
    return pl.pallas_call(
        forward_kernel,
        grid=(count,),
        in_specs=[tok(0), tok(1), tok(2), lane, lane, auxs, state, state, gains],
        out_specs=[tok(0), tok(0), lane, lane, square],
        out_shape=[
            shape((count * tokens, HEAD_DIM), bf16),
            shape((count * tokens, HEAD_DIM), f32),
            shape((SLOTS, count * tokens), f32),
            shape((SLOTS, count * tokens), f32),
            shape((count, tokens, tokens), f32),
        ],
        scratch_shapes=[
            pltpu.VMEM((CHUNK, SLOTS, tokens), f32),
            pltpu.VMEM((CHUNK, tokens), f32),
            pltpu.VMEM((stack, tokens), bf16),
            pltpu.VMEM((stack, tokens), bf16),
        ],
        compiler_params=params(40),
        cost_estimate=cost(count, 1000000000, 3000000),
    )(qkv, qkv, qkv, levels, one, aux, key_in, value_in, gain)


def run_backward(qkv, levels, one, aux, key_in, value_in, gain, mixed, probs, scores, mixed_t, grad_o):
    count, _, tokens = aux.shape
    tok, lane, auxs, state, gains, square, row = seq_specs(tokens)
    stack = big_scratch(tokens)
    return pl.pallas_call(
        backward_kernel,
        grid=(count,),
        in_specs=[tok(0), tok(1), tok(2), lane, lane, auxs, state, state, gains, tok(0), lane, lane, square, tok(0)],
        out_specs=[tok(0), tok(0), tok(0), lane, lane, state, state, row],
        out_shape=[
            shape((count * tokens, HEAD_DIM), bf16),
            shape((count * tokens, HEAD_DIM), f32),
            shape((count * tokens, HEAD_DIM), f32),
            shape((SLOTS, count * tokens), f32),
            shape((SLOTS, count * tokens), f32),
            shape((count, SLOTS, HEAD_DIM), f32),
            shape((count, SLOTS, HEAD_DIM), f32),
            shape((count, 1, HEAD_DIM), f32),
        ],
        scratch_shapes=[
            pltpu.VMEM((CHUNK, SLOTS, tokens), f32),
            pltpu.VMEM((CHUNK, tokens), f32),
            pltpu.VMEM((CHUNK, tokens), f32),
            pltpu.VMEM((stack, tokens), f32),
            pltpu.VMEM((stack, tokens), bf16),
            pltpu.VMEM((stack, tokens), bf16),
        ],
        compiler_params=params(48),
        cost_estimate=cost(count, 3000000000, 5000000),
    )(qkv, qkv, qkv, levels, one, aux, key_in, value_in, gain, mixed, probs, scores, mixed_t, grad_o)


def run_finish(qkv, levels, one, sig, aux, sums, key_in, value_in, key_own, value_own, gk, gv, rows, acts, dk, dv):
    count, _, tokens = aux.shape
    tok, lane, auxs, state, _, square, _ = seq_specs(tokens)
    return pl.pallas_call(
        finish_kernel,
        grid=(count,),
        in_specs=[tok(1), tok(2), lane, lane, lane, auxs, square, state, state, state, state]
        + [tok(0), tok(0), lane, lane, state, state],
        out_specs=[tok(0), tok(0), lane],
        out_shape=[
            shape((count * tokens, HEAD_DIM), bf16),
            shape((count * tokens, HEAD_DIM), bf16),
            shape((SLOTS, count * tokens), bf16),
        ],
        compiler_params=params(40),
        cost_estimate=cost(count, 300000000, 4000000),
    )(qkv, qkv, levels, one, sig, aux, sums, key_in, value_in, key_own, value_own, gk, gv, rows, acts, dk, dv)


def matmul(a, b, ca=1, cb=0):
    return lax.dot_general(a, b, (((ca,), (cb,)), ((), ())), preferred_element_type=f32)


def rms_parts(array, gain_vec):
    factor = lax.rsqrt(jnp.mean(array * array, axis=-1, keepdims=True) + epsilon)
    unit_val = array * factor
    return unit_val, factor, unit_val * gain_vec


def norm_back(unit_val, factor, grad_unit):
    return factor * (grad_unit - unit_val * jnp.mean(grad_unit * unit_val, axis=-1, keepdims=True))


def per_device(
    layer_input, segments, cotangent, norm1_gain, norm2_gain, head_gain, decay_bias,
    w_query, w_key, w_value, w_decay, w_out, w_gate, w_up, w_down,
):
    count, tokens, width = layer_input.shape
    rows = count * tokens
    hidden_units = w_gate.shape[1]
    heads = w_query.shape[1]
    tp_place, here = lax.axis_index("tp"), lax.axis_index("ctx")
    places = lax.axis_size("ctx")
    shard = rows // lax.axis_size("tp")

    def mine(array):
        return lax.dynamic_slice_in_dim(array, tp_place * shard, shard, 0)

    def gather_rows(array):
        return lax.all_gather(array, ("dp", "ctx"), axis=0, tiled=True)

    def scatter_rows(array):
        return lax.psum_scatter(array, ("dp", "ctx"), scatter_dimension=0, tiled=True).astype(f32)

    def to_shards(array):
        return lax.psum_scatter(array.astype(bf16), "tp", scatter_dimension=0, tiled=True).astype(f32)

    def from_shards(array):
        return lax.all_gather(array.astype(bf16), "tp", axis=0, tiled=True)

    w_in = gather_rows(jnp.concatenate([w_query, w_key, w_value, w_decay], axis=1))
    w_rest = gather_rows(jnp.concatenate([w_out.T, w_gate, w_up, w_down.T], axis=1))
    w_qkv, w_dec = w_in[:, : 3 * heads], w_in[:, 3 * heads :]
    w_o = w_rest[:, :heads]
    w_gu = w_rest[:, heads : heads + 2 * hidden_units]
    w_d = w_rest[:, heads + 2 * hidden_units :]

    edges = lax.all_gather(jnp.stack([segments[:, 0], segments[:, -1]]), "ctx")
    prev_doc = jnp.where(here > 0, edges[jnp.maximum(here - 1, 0), 1], -1)
    aux = make_aux(segments, prev_doc)
    place = jnp.arange(tokens)
    sums = (
        (place[:, None] >= place[None, :])[None] & (segments[:, :, None] == segments[:, None, :])
    ).astype(bf16)
    index = jnp.arange(places)
    reach_in = (index[:, None] < here) & (edges[:, 1] == segments[:, 0])
    reach_out = (index[:, None] > here) & (edges[:, 0] == segments[:, -1])
    between = (index[None, :] > jnp.minimum(index[:, None], here)) & (
        index[None, :] < jnp.maximum(index[:, None], here)
    )

    def exchange(keys, values, coefs):
        every = lax.all_gather(jnp.concatenate([keys, values], axis=2), "ctx")
        total = jnp.sum(every * coefs[..., None], axis=0)
        return total[..., :HEAD_DIM], total[..., HEAD_DIM:]

    x = layer_input.reshape(rows, width)
    unit_one, factor_one, scaled_one = rms_parts(x.astype(f32), norm1_gain)
    normed1 = scaled_one.astype(bf16)
    qkv = matmul(normed1, w_qkv).astype(bf16)
    bias_here = lax.dynamic_slice_in_dim(decay_bias, tp_place * SLOTS, SLOTS)
    logits = matmul(w_dec, normed1, 0, 1) + bias_here[:, None]
    log_decay = jax.nn.log_sigmoid(logits) / gate_norm
    one = -jnp.expm1(log_decay)
    sig = jax.nn.sigmoid(-logits) / gate_norm
    levels, key_own, value_own = run_states(qkv, log_decay, one, aux)
    ends = lax.all_gather(levels[:, tokens - 1 :: tokens].T, "ctx")
    span = jnp.exp(jnp.sum(jnp.where(between[:, :, None, None], ends[None], 0.0), axis=1))
    coef_in = jnp.where(reach_in[..., None], span, 0.0)
    coef_out = jnp.where(reach_out[..., None], span, 0.0)
    key_in, value_in = exchange(key_own, value_own, coef_in)
    gain = head_gain[None, :]
    normed_o, mixed, probs, scores, mixed_t = run_forward(
        qkv, levels, one, aux, key_in, value_in, gain
    )
    hidden = mine(x).astype(f32) + to_shards(matmul(normed_o, w_o, 1, 1))
    unit_two, factor_two, scaled_two = rms_parts(hidden, norm2_gain)
    normed2 = from_shards(scaled_two)
    pre = matmul(normed2, w_gu)
    gate_pre, up_pre = pre[:, :hidden_units], pre[:, hidden_units:]
    gate_sig = jax.nn.sigmoid(gate_pre)
    gate_silu = gate_pre * gate_sig
    hidden_act = (gate_silu * up_pre).astype(bf16)
    feed = to_shards(matmul(hidden_act, w_d, 1, 1))
    output = from_shards(hidden + feed)

    grad_feed = cotangent.reshape(rows, width)
    grad_act = matmul(grad_feed, w_d)
    grad_gate = (grad_act * up_pre * gate_sig * (1.0 + gate_pre * (1.0 - gate_sig))).astype(bf16)
    grad_up = (grad_act * gate_silu).astype(bf16)
    grad_gu = jnp.concatenate([grad_gate, grad_up], axis=1)
    grad_n2 = to_shards(matmul(grad_gu, w_gu, 1, 1))
    grad_wgu = matmul(normed2, grad_gu, 0, 0).astype(bf16)
    grad_wd = matmul(grad_feed, hidden_act, 0, 0).astype(bf16)
    ffn_rows = scatter_rows(jnp.concatenate([grad_wgu, grad_wd], axis=1))
    gain_two_part = jnp.sum(grad_n2 * unit_two, axis=0)
    grad_hidden = mine(grad_feed).astype(f32) + norm_back(unit_two, factor_two, grad_n2 * norm2_gain)
    grad_attn = from_shards(grad_hidden)
    grad_o = matmul(grad_attn, w_o)
    grad_wo = matmul(grad_attn, normed_o, 0, 0).astype(bf16)
    grad_q, gk, gv, row_sums, acts, dk, dv, head_part = run_backward(
        qkv, levels, one, aux, key_in, value_in, gain, mixed, probs, scores, mixed_t, grad_o
    )
    dk_later, dv_later = exchange(dk, dv, coef_out)
    grad_k, grad_v, grad_logits = run_finish(
        qkv, levels, one, sig, aux, sums, key_in, value_in, key_own, value_own,
        gk, gv, row_sums, acts, dk_later, dv_later,
    )
    grad_all = jnp.concatenate([grad_q, grad_k, grad_v, grad_logits.T], axis=1)
    grad_n1 = to_shards(matmul(grad_all, w_in, 1, 1))
    grad_in = matmul(normed1, grad_all, 0, 0).astype(bf16)
    att_rows = scatter_rows(jnp.concatenate([grad_in, grad_wo], axis=1))
    unit_mine, factor_mine = mine(unit_one), mine(factor_one)
    gain_one_part = jnp.sum(grad_n1 * unit_mine, axis=0)
    input_grad = grad_hidden + norm_back(unit_mine, factor_mine, grad_n1 * norm1_gain)
    input_grad = from_shards(input_grad).astype(f32)
    bias_part = lax.dynamic_update_slice_in_dim(
        jnp.zeros_like(decay_bias),
        jnp.sum(grad_logits.astype(f32), axis=1),
        tp_place * SLOTS,
        0,
    )
    small = lax.psum(
        jnp.concatenate([gain_one_part, gain_two_part, jnp.sum(head_part, axis=(0, 1)), bias_part]),
        ("dp", "ctx", "tp"),
    )
    cut = 3 * heads
    return (
        output.reshape(count, tokens, width),
        input_grad.reshape(count, tokens, width),
        small[:width],
        small[width : 2 * width],
        small[2 * width : 2 * width + HEAD_DIM],
        small[2 * width + HEAD_DIM :],
        att_rows[:, :heads],
        att_rows[:, heads : 2 * heads],
        att_rows[:, 2 * heads : cut],
        att_rows[:, cut : cut + SLOTS],
        att_rows[:, cut + SLOTS :].T,
        ffn_rows[:, :hidden_units],
        ffn_rows[:, hidden_units : 2 * hidden_units],
        ffn_rows[:, 2 * hidden_units :].T,
    )


def solution(mesh):
    return jax.shard_map(
        per_device,
        mesh=mesh,
        in_specs=(
            P("dp", "ctx", None),
            P("dp", "ctx"),
            P("dp", "ctx", None),
            P(),
            P(),
            P(),
            P(),
            P(("dp", "ctx"), "tp"),
            P(("dp", "ctx"), "tp"),
            P(("dp", "ctx"), "tp"),
            P(("dp", "ctx"), "tp"),
            P("tp", ("dp", "ctx")),
            P(("dp", "ctx"), "tp"),
            P(("dp", "ctx"), "tp"),
            P("tp", ("dp", "ctx")),
        ),
        out_specs=(
            P("dp", "ctx", None),
            P("dp", "ctx", None),
            P(),
            P(),
            P(),
            P(),
            P(("dp", "ctx"), "tp"),
            P(("dp", "ctx"), "tp"),
            P(("dp", "ctx"), "tp"),
            P(("dp", "ctx"), "tp"),
            P("tp", ("dp", "ctx")),
            P(("dp", "ctx"), "tp"),
            P(("dp", "ctx"), "tp"),
            P("tp", ("dp", "ctx")),
        ),
        check_vma=False,
    )
```

```python
import jax
import jax.numpy as jnp
from jax import lax
from jax.experimental import pallas as pl
from jax.experimental.layout import Layout, with_layout_constraint
from jax.experimental.pallas import tpu as pltpu
from jax.sharding import PartitionSpec as P

HEAD_DIM = 512
SLOTS = 64
CHUNK = 32
epsilon = 1e-05
gate_norm = 8.0
f32 = jnp.float32
bf16 = jnp.bfloat16
NEG = -1e30
SCALE = HEAD_DIM**-0.5


def split2(x):
    high = x.astype(bf16)
    return high, (x - high.astype(f32)).astype(bf16)


def dg(a, b, ca, cb):
    return lax.dot_general(a, b, (((ca,), (cb,)), ((), ())), preferred_element_type=f32)


def dot2(a, b, ca, cb):
    high, low = a
    return dg(high, b, ca, cb) + dg(low, b, ca, cb)


def dot2r(a, b, ca, cb):
    high, low = b
    return dg(a, high, ca, cb) + dg(a, low, ca, cb)


def dot3(a, b, ca, cb):
    return dg(a[0], b[0], ca, cb) + (dg(a[0], b[1], ca, cb) + dg(a[1], b[0], ca, cb))


def group_lane(x, index):
    rows, lanes = x.shape
    lane = lax.broadcasted_iota(jnp.int32, (rows, 128), 1)
    at = (lane // CHUNK) * CHUNK + index
    parts = [
        jnp.take_along_axis(x[:, i : i + 128], at, axis=1, mode="promise_in_bounds")
        for i in range(0, lanes, 128)
    ]
    return jnp.concatenate(parts, axis=1)


def chunk_of(rows, lanes):
    return lax.broadcasted_iota(jnp.int32, (rows, lanes), 1) // CHUNK


def pick_rows(array, rows, chunks, first=0):
    lanes = array.shape[1]
    chunk = chunk_of(rows, lanes)
    total = jnp.zeros((rows, lanes), f32)
    for c in range(first, chunks):
        total = jnp.where(chunk == c, array[(c - first) * rows : (c - first + 1) * rows], total)
    return total


def level_refs(levels):
    slots, tokens = levels.shape
    chunk = chunk_of(slots, tokens)
    refs = jnp.zeros_like(levels)
    for c in range(1, tokens // CHUNK):
        refs = jnp.where(chunk == c, levels[:, c * CHUNK - 1 : c * CHUNK], refs)
    return refs


def stack_chunks(array, chunks):
    chunk = chunk_of(*array.shape)
    return jnp.concatenate([jnp.where(chunk == c, array, 0.0) for c in range(1, chunks)], axis=0)


def rows_of(ref):
    return ref[...].reshape(-1, ref.shape[-1])


def store_rows(ref, value):
    ref[...] = value.reshape(ref.shape)


def aux_rows(tokens):
    chunks = tokens // CHUNK
    base = 2 * CHUNK + chunks
    return base, base + 8


def make_aux(seg, prev_doc):
    count, tokens = seg.shape
    chunks = tokens // CHUNK
    place = jnp.arange(tokens)
    local = place % CHUNK
    grouped = seg.reshape(count, chunks, CHUNK)
    spread = jnp.repeat(grouped.transpose(0, 2, 1), CHUNK, axis=2)
    index = jnp.arange(CHUNK)[:, None]
    same = spread == seg[:, None, :]
    from_j = same & (local[None, :] >= index)[None]
    to_i = same & (local[None, :] <= index)[None]
    ends = jnp.concatenate([jnp.full((count, 1), -5, seg.dtype), grouped[:, :-1, -1]], axis=1)
    before = (ends[:, :, None] == seg[:, None, :]) & (
        place[None, :] < (jnp.arange(chunks) * CHUNK)[:, None]
    )[None]
    after = jnp.repeat(ends, CHUNK, axis=1) == seg
    first = seg == seg[:, :1]
    last = seg == seg[:, -1:]
    bias = jnp.concatenate(
        [from_j, to_i, before, after[:, None], first[:, None], last[:, None]], axis=1
    )
    bias = jnp.where(bias, 0.0, NEG).astype(f32)
    previous = jnp.concatenate([prev_doc[:, None], seg[:, :-1]], axis=1)
    keeps = (previous == seg).astype(f32)[:, None]
    pad = jnp.zeros((count, 4, tokens), f32)
    return jnp.concatenate([bias, keeps, pad], axis=1)


def state_kernel(k_ref, v_ref, ld_ref, one_ref, aux_ref, lev_ref, ks_ref, vs_ref):
    tokens = ld_ref.shape[1]
    base, _ = aux_rows(tokens)
    earlier = lax.broadcasted_iota(jnp.int32, (tokens, tokens), 0)
    later = lax.broadcasted_iota(jnp.int32, (tokens, tokens), 1)
    upper = jnp.where(earlier <= later, 1.0, 0.0).astype(bf16)
    ld = ld_ref[...]
    high, rest = ld.astype(bf16), None
    rest = ld - high.astype(f32)
    mid, low = split2(rest)
    levels = dg(high, upper, 1, 0) + (dg(mid, upper, 1, 0) + dg(low, upper, 1, 0))
    lev_ref[...] = levels
    tail = jnp.exp(levels[:, tokens - 1 : tokens] - levels + aux_ref[0, base + 2 : base + 3, :])
    tail = split2(tail * one_ref[...])
    ks_ref[0] = dot2(tail, rows_of(k_ref), 1, 0)
    vs_ref[0] = dot2(tail, rows_of(v_ref), 1, 0)


def forward_kernel(
    q_ref, k_ref, v_ref, lev_ref, one_ref, aux_ref, ki_ref, vi_ref, gain_ref,
    no_ref, mix_ref, p_ref, sc_ref, mt_ref, w_scr, d_scr, wh_scr, wl_scr,
):
    tokens = lev_ref.shape[1]
    chunks = tokens // CHUNK
    base, _ = aux_rows(tokens)
    levels, one = lev_ref[...], one_ref[...]
    q, k, v = rows_of(q_ref), rows_of(k_ref), rows_of(v_ref)
    chunk = chunk_of(SLOTS, tokens)
    kq = dg(k, q, 1, 1)
    d_scr[...] = pick_rows(kq, CHUNK, chunks)

    def inside(j, scores):
        gap = levels - group_lane(levels, j) + aux_ref[0, pl.ds(j, 1), :]
        w = jnp.exp(gap) * group_lane(one, j)
        w_scr[j] = w
        return scores + w * d_scr[pl.ds(j, 1), :]

    scores = lax.fori_loop(0, CHUNK, inside, jnp.zeros_like(levels), unroll=2)
    decay = jnp.exp(levels - level_refs(levels) + aux_ref[0, base : base + 1, :])
    for c in range(1, chunks):
        w = levels[:, c * CHUNK - 1 : c * CHUNK] - levels + aux_ref[0, 2 * CHUNK + c : 2 * CHUNK + c + 1, :]
        wh, wl = split2(jnp.exp(w) * one)
        wh_scr[(c - 1) * SLOTS : c * SLOTS] = wh
        wl_scr[(c - 1) * SLOTS : c * SLOTS] = wl
    wst = (wh_scr[...], wl_scr[...])
    scores += decay * pick_rows(dot3(wst, split2(kq), 1, 0), SLOTS, chunks, 1)
    carried = jnp.exp(levels + aux_ref[0, base + 1 : base + 2, :])
    scores += carried * dot2(split2(ki_ref[0]), q, 1, 1)
    sc_ref[...] = scores
    z = scores * SCALE
    e = jnp.exp(z - jnp.max(z, axis=0, keepdims=True))
    probs = e / jnp.sum(e, axis=0, keepdims=True)
    p_ref[...] = probs

    def mixing(j, carry):
        d_scr[pl.ds(j, 1), :] = jnp.sum(w_scr[j] * probs, axis=0, keepdims=True)
        return carry

    lax.fori_loop(0, CHUNK, mixing, 0, unroll=2)
    row = lax.broadcasted_iota(jnp.int32, (tokens, tokens), 0) // CHUNK
    col = lax.broadcasted_iota(jnp.int32, (tokens, tokens), 1) // CHUNK
    mixed_t = jnp.where(row == col, jnp.concatenate([d_scr[...]] * chunks, axis=0), 0.0)
    mixed_t += dot3(wst, split2(stack_chunks(probs * decay, chunks)), 0, 0)
    mt_ref[0] = mixed_t
    out = dot2(split2(mixed_t), v, 0, 0) + dot3(split2(probs * carried), split2(vi_ref[0]), 0, 0)
    mix_ref[...] = out
    unit = out * lax.rsqrt(jnp.mean(out * out, axis=1, keepdims=True) + epsilon)
    store_rows(no_ref, (unit * gain_ref[...]).astype(bf16))


def backward_kernel(
    q_ref, k_ref, v_ref, lev_ref, one_ref, aux_ref, ki_ref, vi_ref, gain_ref, mix_ref, p_ref, sc_ref, mt_ref, go_ref,
    gq_ref, gk_ref, gv_ref, r_ref, a_ref, dk_ref, dv_ref, hg_ref, w_scr, d_scr, e_scr, x_scr, wh_scr, wl_scr,
):
    tokens = lev_ref.shape[1]
    chunks = tokens // CHUNK
    base, _ = aux_rows(tokens)
    levels, one, probs = lev_ref[...], one_ref[...], p_ref[...]
    q, k, v = rows_of(q_ref), rows_of(k_ref), rows_of(v_ref)
    out, go = mix_ref[...], rows_of(go_ref)
    factor = lax.rsqrt(jnp.mean(out * out, axis=1, keepdims=True) + epsilon)
    unit = out * factor
    hg_ref[0] = jnp.sum(go * unit, axis=0, keepdims=True)
    go = go * gain_ref[...]
    grad = factor * (go - unit * jnp.mean(go * unit, axis=1, keepdims=True))
    g = split2(grad)
    kin, vin = split2(ki_ref[0]), split2(vi_ref[0])
    gv = dot2r(v, g, 1, 1)
    d_scr[...] = pick_rows(gv, CHUNK, chunks)

    def inside(j, dp):
        gap = levels - group_lane(levels, j) + aux_ref[0, pl.ds(j, 1), :]
        w = jnp.exp(gap) * group_lane(one, j)
        w_scr[j] = w
        return dp + w * d_scr[pl.ds(j, 1), :]

    dp = lax.fori_loop(0, CHUNK, inside, jnp.zeros_like(levels), unroll=2)
    decay = jnp.exp(levels - level_refs(levels) + aux_ref[0, base : base + 1, :])
    for c in range(1, chunks):
        w = levels[:, c * CHUNK - 1 : c * CHUNK] - levels + aux_ref[0, 2 * CHUNK + c : 2 * CHUNK + c + 1, :]
        w = jnp.exp(w)
        x_scr[(c - 1) * SLOTS : c * SLOTS] = w
        wh, wl = split2(w * one)
        wh_scr[(c - 1) * SLOTS : c * SLOTS] = wh
        wl_scr[(c - 1) * SLOTS : c * SLOTS] = wl
    wst = (wh_scr[...], wl_scr[...])
    dp += decay * pick_rows(dot3(wst, split2(gv), 1, 0), SLOTS, chunks, 1)
    carried = jnp.exp(levels + aux_ref[0, base + 1 : base + 2, :])
    dp += carried * dot3(vin, g, 1, 1)
    dz = SCALE * probs * (dp - jnp.sum(probs * dp, axis=0, keepdims=True))
    a_ref[...] = dz * sc_ref[...] + probs * dp

    def mixing(j, carry):
        d_scr[pl.ds(j, 1), :] = jnp.sum(w_scr[j] * dz, axis=0, keepdims=True)
        return carry

    lax.fori_loop(0, CHUNK, mixing, 0, unroll=2)
    row = lax.broadcasted_iota(jnp.int32, (tokens, tokens), 0) // CHUNK
    col = lax.broadcasted_iota(jnp.int32, (tokens, tokens), 1) // CHUNK
    mz_t = jnp.where(row == col, jnp.concatenate([d_scr[...]] * chunks, axis=0), 0.0)
    zst = split2(stack_chunks(dz * decay, chunks))
    pst = split2(stack_chunks(probs * decay, chunks))
    mz_t += dot3(wst, zst, 0, 0)
    mz = split2(mz_t)
    zc, pc = split2(dz * carried), split2(probs * carried)
    store_rows(gq_ref, (dot2(mz, k, 0, 0) + dot3(zc, kin, 0, 0)).astype(bf16))
    gk_ref[...] = dot2(mz, q, 1, 0)
    gv_ref[...] = dot3(split2(mt_ref[0]), g, 1, 0)
    dk_ref[0] = dot2(zc, q, 1, 0)
    dv_ref[0] = dot3(pc, g, 1, 0)
    qk = dg(q, k, 1, 1)
    gv_n = dot2(g, v, 1, 1)
    d_scr[...] = pick_rows(qk, CHUNK, chunks)
    e_scr[...] = pick_rows(gv_n, CHUNK, chunks)

    def onward(i, total):
        gap = group_lane(levels, i) - levels + aux_ref[0, pl.ds(CHUNK + i, 1), :]
        term = group_lane(dz, i) * d_scr[pl.ds(i, 1), :] + group_lane(probs, i) * e_scr[pl.ds(i, 1), :]
        return total + jnp.exp(gap) * term

    total = lax.fori_loop(0, CHUNK, onward, jnp.zeros_like(levels), unroll=2)
    cross = dot3(zst, split2(qk), 1, 0) + dot3(pst, split2(gv_n), 1, 0)
    for c in range(1, chunks):
        total += x_scr[(c - 1) * SLOTS : c * SLOTS] * cross[(c - 1) * SLOTS : c * SLOTS]
    r_ref[...] = total


def finish_kernel(
    k_ref, v_ref, lev_ref, one_ref, sig_ref, aux_ref, sums_ref, ki_ref, vi_ref, ks_ref, vs_ref, gk_ref, gv_ref,
    r_ref, a_ref, dk_ref, dv_ref, gko_ref, gvo_ref, gl_ref,
):
    tokens = lev_ref.shape[1]
    base, _ = aux_rows(tokens)
    levels, one = lev_ref[...], one_ref[...]
    k, v = rows_of(k_ref), rows_of(v_ref)
    tail = jnp.exp(levels[:, tokens - 1 : tokens] - levels + aux_ref[0, base + 2 : base + 3, :])
    end = jnp.exp(levels[:, tokens - 1 : tokens] + aux_ref[0, base + 1 : base + 2, tokens - 1 : tokens])
    dk, dv = dk_ref[0], dv_ref[0]
    dks, dvs = split2(dk), split2(dv)
    weights = split2(tail * one)
    store_rows(gko_ref, (gk_ref[...] + dot3(weights, dks, 0, 0)).astype(bf16))
    store_rows(gvo_ref, (gv_ref[...] + dot3(weights, dvs, 0, 0)).astype(bf16))
    rows = r_ref[...] + tail * (dot2(dks, k, 1, 1) + dot2(dvs, v, 1, 1))
    final_k = end * ki_ref[0] + ks_ref[0]
    final_v = end * vi_ref[0] + vs_ref[0]
    at_end = jnp.sum(dk * final_k + dv * final_v, axis=1, keepdims=True)
    x = a_ref[...] - one * rows
    high = x.astype(bf16)
    mid, low = split2(x - high.astype(f32))
    sums = sums_ref[0]
    flow = dg(high, sums, 1, 0) + (dg(mid, sums, 1, 0) + dg(low, sums, 1, 0))
    flow += jnp.where(aux_ref[0, base + 2 : base + 3, :] == 0.0, at_end, 0.0)
    grad = flow * aux_ref[0, base + 3 : base + 4, :] - (1.0 - one) * rows
    gl_ref[...] = (grad * sig_ref[...]).astype(bf16)


def seq_specs(tokens, members):
    def own(col):
        return pl.BlockSpec((members, 1, tokens // members, HEAD_DIM), lambda i: (0, i, 0, col))

    tok = pl.BlockSpec((tokens, HEAD_DIM), lambda i: (i, 0))
    lane = pl.BlockSpec((SLOTS, tokens), lambda i: (0, i))
    _, rows = aux_rows(tokens)
    aux = pl.BlockSpec((1, rows, tokens), lambda i: (i, 0, 0))
    state = pl.BlockSpec((1, SLOTS, HEAD_DIM), lambda i: (i, 0, 0))
    gain = pl.BlockSpec((1, HEAD_DIM), lambda i: (0, 0))
    square = pl.BlockSpec((1, tokens, tokens), lambda i: (i, 0, 0))
    row = pl.BlockSpec((1, 1, HEAD_DIM), lambda i: (i, 0, 0))
    return own, tok, lane, aux, state, gain, square, row


def params(mib):
    return pltpu.CompilerParams(vmem_limit_bytes=mib << 20)


def cost(count, flops, size):
    return pl.CostEstimate(flops=count * flops, bytes_accessed=count * size, transcendentals=count * 1000000)


def shape(dims, dtype):
    return jax.ShapeDtypeStruct(dims, dtype)


def run_states(qkv, ld, one, aux):
    count, _, tokens = aux.shape
    own, tok, lane, auxs, state, _, _, _ = seq_specs(tokens, qkv.shape[0])
    return pl.pallas_call(
        state_kernel,
        grid=(count,),
        in_specs=[own(1), own(2), lane, lane, auxs],
        out_specs=[lane, state, state],
        out_shape=[
            shape((SLOTS, count * tokens), f32),
            shape((count, SLOTS, HEAD_DIM), f32),
            shape((count, SLOTS, HEAD_DIM), f32),
        ],
        compiler_params=params(24),
        cost_estimate=cost(count, 100000000, 1500000),
    )(qkv, qkv, ld, one, aux)


def big_scratch(tokens):
    stack = (tokens // CHUNK - 1) * SLOTS
    return stack


def run_forward(qkv, levels, one, aux, key_in, value_in, gain):
    count, _, tokens = aux.shape
    own, tok, lane, auxs, state, gains, square, _ = seq_specs(tokens, qkv.shape[0])
    stack = big_scratch(tokens)
    return pl.pallas_call(
        forward_kernel,
        grid=(count,),
        in_specs=[own(0), own(1), own(2), lane, lane, auxs, state, state, gains],
        out_specs=[own(0), tok, lane, lane, square],
        out_shape=[
            shape(qkv.shape[:3] + (HEAD_DIM,), bf16),
            shape((count * tokens, HEAD_DIM), f32),
            shape((SLOTS, count * tokens), f32),
            shape((SLOTS, count * tokens), f32),
            shape((count, tokens, tokens), f32),
        ],
        scratch_shapes=[
            pltpu.VMEM((CHUNK, SLOTS, tokens), f32),
            pltpu.VMEM((CHUNK, tokens), f32),
            pltpu.VMEM((stack, tokens), bf16),
            pltpu.VMEM((stack, tokens), bf16),
        ],
        compiler_params=params(40),
        cost_estimate=cost(count, 1000000000, 3000000),
    )(qkv, qkv, qkv, levels, one, aux, key_in, value_in, gain)


def run_backward(qkv, levels, one, aux, key_in, value_in, gain, mixed, probs, scores, mixed_t, grad_o):
    count, _, tokens = aux.shape
    own, tok, lane, auxs, state, gains, square, row = seq_specs(tokens, qkv.shape[0])
    stack = big_scratch(tokens)
    return pl.pallas_call(
        backward_kernel,
        grid=(count,),
        in_specs=[own(0), own(1), own(2), lane, lane, auxs, state, state, gains, tok, lane, lane, square, own(0)],
        out_specs=[own(0), tok, tok, lane, lane, state, state, row],
        out_shape=[
            shape(qkv.shape[:3] + (HEAD_DIM,), bf16),
            shape((count * tokens, HEAD_DIM), f32),
            shape((count * tokens, HEAD_DIM), f32),
            shape((SLOTS, count * tokens), f32),
            shape((SLOTS, count * tokens), f32),
            shape((count, SLOTS, HEAD_DIM), f32),
            shape((count, SLOTS, HEAD_DIM), f32),
            shape((count, 1, HEAD_DIM), f32),
        ],
        scratch_shapes=[
            pltpu.VMEM((CHUNK, SLOTS, tokens), f32),
            pltpu.VMEM((CHUNK, tokens), f32),
            pltpu.VMEM((CHUNK, tokens), f32),
            pltpu.VMEM((stack, tokens), f32),
            pltpu.VMEM((stack, tokens), bf16),
            pltpu.VMEM((stack, tokens), bf16),
        ],
        compiler_params=params(48),
        cost_estimate=cost(count, 3000000000, 5000000),
    )(qkv, qkv, qkv, levels, one, aux, key_in, value_in, gain, mixed, probs, scores, mixed_t, grad_o)


def run_finish(qkv, levels, one, sig, aux, sums, key_in, value_in, key_own, value_own, gk, gv, rows, acts, dk, dv):
    count, _, tokens = aux.shape
    own, tok, lane, auxs, state, _, square, _ = seq_specs(tokens, qkv.shape[0])
    return pl.pallas_call(
        finish_kernel,
        grid=(count,),
        in_specs=[own(1), own(2), lane, lane, lane, auxs, square, state, state, state, state]
        + [tok, tok, lane, lane, state, state],
        out_specs=[own(0), own(0), lane],
        out_shape=[
            shape(qkv.shape[:3] + (HEAD_DIM,), bf16),
            shape(qkv.shape[:3] + (HEAD_DIM,), bf16),
            shape((SLOTS, count * tokens), bf16),
        ],
        compiler_params=params(40),
        cost_estimate=cost(count, 300000000, 4000000),
    )(qkv, qkv, levels, one, sig, aux, sums, key_in, value_in, key_own, value_own, gk, gv, rows, acts, dk, dv)


def matmul(a, b, ca=1, cb=0):
    return lax.dot_general(a, b, (((ca,), (cb,)), ((), ())), preferred_element_type=f32)


def rms_parts(array, gain_vec):
    factor = lax.rsqrt(jnp.mean(array * array, axis=-1, keepdims=True) + epsilon)
    unit_val = array * factor
    return unit_val, factor, unit_val * gain_vec


def norm_back(unit_val, factor, grad_unit):
    return factor * (grad_unit - unit_val * jnp.mean(grad_unit * unit_val, axis=-1, keepdims=True))


def row_major(array):
    return with_layout_constraint(array, Layout(major_to_minor=tuple(range(array.ndim))))


def after(values, *events):
    return lax.optimization_barrier((values, events))[0]


def line_gather(own, axis, put, buffer):
    size, here = lax.axis_size(axis), lax.axis_index(axis)
    for step_to in (1, -1):
        moving = own
        for s in range(1, size):
            sources = range(s - 1, size - 1) if step_to == 1 else range(1, size - s + 1)
            moving = lax.ppermute(moving, axis, [(i, i + step_to) for i in sources])
            origin = here - s * step_to
            valid = (origin >= 0) & (origin < size)
            buffer = put(buffer, moving, jnp.where(valid, origin, here))
    return put(buffer, own, here)


def per_device(
    layer_input, segments, cotangent, norm1_gain, norm2_gain, head_gain, decay_bias,
    w_query, w_key, w_value, w_decay, w_out, w_gate, w_up, w_down,
):
    count, tokens, width = layer_input.shape
    rows = count * tokens
    hidden_units = w_gate.shape[1]
    heads = w_query.shape[1]
    tp_place, here = lax.axis_index("tp"), lax.axis_index("ctx")
    swap_x = [(0, 1), (1, 0), (2, 3), (3, 2)]
    places, members = lax.axis_size("ctx"), lax.axis_size("tp")
    part = tokens // members

    def owner_first(array):
        array = array.reshape(count, members, part, width).transpose(1, 0, 2, 3)
        return array.reshape(rows, width)

    def natural(array):
        return array.reshape(members, count, part, width).transpose(1, 0, 2, 3)

    def lanes(array, order):
        array = array.reshape(array.shape[0], *order, part).transpose(0, 2, 1, 3)
        return array.reshape(array.shape[0], rows)

    def blocks_of(array):
        return array.reshape(members, count, part, -1)

    def mine(array):
        return lax.dynamic_slice_in_dim(array, tp_place * (count * part), count * part, 0)

    def to_shards(array):
        return lax.psum_scatter(array, "tp", scatter_dimension=0, tiled=True).astype(f32)

    def from_shards(array):
        return lax.all_gather(array.astype(bf16), "tp", axis=0, tiled=True)

    def gather_rows(array):
        return lax.all_gather(array, ("dp", "ctx"), axis=0, tiled=True)

    def scatter_rows(array, wait=None):
        if places != 4:
            return lax.psum_scatter(
                array, ("dp", "ctx"), scatter_dimension=0, tiled=True
            ).astype(f32), ()
        core, y, x = lax.axis_index("dp"), here // 2, here % 2
        size, cols = array.shape[0] // 8, array.shape[1]
        half = size // 2

        def pick(value, index, axis):
            return lax.dynamic_index_in_dim(value, index, axis, keepdims=False)

        def add(a, b, dtype=bf16):
            return (a.astype(f32) + b.astype(f32)).astype(dtype)

        swap_y = [(0, 2), (2, 0), (1, 3), (3, 1)]
        array = row_major(array).reshape(2, 2, 2, size, cols)
        other = lax.ppermute(pick(array, 1 - core, 0), "dp", [(0, 1), (1, 0)])
        chip = add(pick(array, core, 0), other)
        over_x = lax.ppermute(pick(chip[:, :, :half], 1 - x, 1), "ctx", swap_x)
        over_y = lax.ppermute(pick(chip[:, :, half:], 1 - y, 0), "ctx", swap_y)
        upper = add(pick(chip[:, :, :half], x, 1), over_x)
        lower = add(pick(chip[:, :, half:], y, 0), over_y)
        last_y = lax.ppermute(pick(upper, 1 - y, 0), "ctx", swap_y)
        last_x = lax.ppermute(pick(lower, 1 - x, 0), "ctx", swap_x)
        upper = add(pick(upper, y, 0), last_y, f32)
        lower = add(pick(lower, x, 0), last_x, f32)
        return jnp.concatenate([upper, lower], axis=0), (chip, upper, lower)

    def gather_in_parts(array, parts):
        buffer = jnp.zeros((members, parts, count * part // parts, width), bf16)
        for c, block in enumerate(array.astype(bf16).reshape(buffer.shape[1:])):

            def put(buf, value, owner, c=c):
                return lax.dynamic_update_slice(buf, value[None, None], (owner, c, 0, 0))

            buffer = line_gather(block, "tp", put, buffer)
        return buffer.reshape(rows, width)

    def from_partner(array, distance):
        return lax.ppermute(array, "tp", [(i, i ^ distance) for i in range(members)])

    def sum_small(array):
        if places != 4:
            return lax.psum(array, ("dp", "ctx", "tp"))
        array += lax.ppermute(array, "dp", [(0, 1), (1, 0)])
        for axis in ("ctx", "tp"):
            for r in (1, 2):
                array += lax.ppermute(array, axis, [(i, i ^ r) for i in range(4)])
        return array

    cut = 3 * heads
    w_in = gather_rows(jnp.concatenate([w_query, w_key, w_value, w_decay], axis=1))
    w_qkv, w_dec = w_in[:, :cut], w_in[:, cut:]
    w_out_t = w_out.T
    w_heads = gather_rows(
        jnp.concatenate([w_out_t] + [from_partner(w_out_t, r) for r in range(1, members)], axis=1)
    )
    w_o = w_heads[:, :heads]
    w_rest = gather_rows(jnp.concatenate([w_gate, w_up, w_down.T], axis=1))
    w_gu = w_rest[:, : 2 * hidden_units]
    w_d = w_rest[:, 2 * hidden_units :]

    edges = lax.all_gather(jnp.stack([segments[:, 0], segments[:, -1]]), "ctx")
    prev_doc = jnp.where(here > 0, edges[jnp.maximum(here - 1, 0), 1], -1)
    aux = make_aux(segments, prev_doc)
    place = jnp.arange(tokens)
    sums = (
        (place[:, None] >= place[None, :])[None] & (segments[:, :, None] == segments[:, None, :])
    ).astype(bf16)
    index = jnp.arange(places)
    reach_in = (index[:, None] < here) & (edges[:, 1] == segments[:, 0])
    reach_out = (index[:, None] > here) & (edges[:, 0] == segments[:, -1])
    between = (index[None, :] > jnp.minimum(index[:, None], here)) & (
        index[None, :] < jnp.maximum(index[:, None], here)
    )

    square = places == 4
    if square:
        low = 2 * (here // 2)
        is_low = here == low

        def exchange(keys, values, coefs, forward, own_end, near_end):
            own = jnp.concatenate([keys, values], axis=2)
            near = lax.ppermute(own.astype(bf16), "ctx", swap_x).astype(f32)
            first, second = jnp.where(is_low, own, near), jnp.where(is_low, near, own)
            low_end, high_end = jnp.where(is_low, own_end, near_end), jnp.where(is_low, near_end, own_end)
            if forward:
                link = lax.dynamic_index_in_dim(edges, low, 0, False)[1] == lax.dynamic_index_in_dim(edges, low + 1, 0, False)[1]
                joined = second + jnp.where(link[:, None], jnp.exp(high_end), 0.0)[..., None] * first
                pairs, origin = [(0, 2), (1, 3)], 1
            else:
                link = lax.dynamic_index_in_dim(edges, low, 0, False)[0] == lax.dynamic_index_in_dim(edges, low + 1, 0, False)[0]
                joined = first + jnp.where(link[:, None], jnp.exp(low_end), 0.0)[..., None] * second
                pairs, origin = [(2, 0), (3, 1)], 2
            far = lax.ppermute(joined.astype(bf16), "ctx", pairs).astype(f32)
            beside = lax.dynamic_index_in_dim(coefs, here + jnp.where(is_low, 1, -1), 0, False)
            total = beside[..., None] * near + coefs[origin][..., None] * far
            return total[..., :HEAD_DIM], total[..., HEAD_DIM:]

        def level_ends(own_end):
            near_end = lax.ppermute(own_end, "ctx", swap_x)
            slot = (index == here)[:, None, None]
            beside = (index == here + jnp.where(is_low, 1, -1))[:, None, None]
            return jnp.where(slot, own_end, 0.0) + jnp.where(beside, near_end, 0.0), near_end

    else:

        def exchange(keys, values, coefs, forward, own_end, near_end):
            every = lax.all_gather(jnp.concatenate([keys, values], axis=2), "ctx")
            total = jnp.sum(every * coefs[..., None], axis=0)
            return total[..., :HEAD_DIM], total[..., HEAD_DIM:]

        def level_ends(own_end):
            return lax.all_gather(own_end, "ctx"), own_end

    x = owner_first(layer_input)
    unit_one, factor_one, scaled_one = rms_parts(x.astype(f32), norm1_gain)
    normed1 = scaled_one.astype(bf16)
    qkv = blocks_of(matmul(normed1, w_qkv).astype(bf16))
    bias_here = lax.dynamic_slice_in_dim(decay_bias, tp_place * SLOTS, SLOTS)
    logits = lanes(matmul(w_dec, normed1, 0, 1), (members, count)) + bias_here[:, None]
    log_decay = jax.nn.log_sigmoid(logits) / gate_norm
    one = -jnp.expm1(log_decay)
    sig = jax.nn.sigmoid(-logits) / gate_norm
    levels, key_own, value_own = run_states(qkv, log_decay, one, aux)
    own_end = levels[:, tokens - 1 :: tokens].T
    ends, near_end = level_ends(own_end)
    span = jnp.exp(jnp.sum(jnp.where(between[:, :, None, None], ends[None], 0.0), axis=1))
    coef_in = jnp.where(reach_in[..., None], span, 0.0)
    coef_out = jnp.where(reach_out[..., None], span, 0.0)
    key_in, value_in = exchange(key_own, value_own, coef_in, True, own_end, near_end)
    gain = head_gain[None, :]
    normed_o, mixed, probs, scores, mixed_t = run_forward(
        qkv, levels, one, aux, key_in, value_in, gain
    )
    by_owner = normed_o.reshape(members, count * part, heads)

    def for_partner(r):
        return lax.dynamic_index_in_dim(by_owner, tp_place ^ r, 0, keepdims=False)

    normed_heads = jnp.concatenate(
        [for_partner(0)] + [from_partner(for_partner(r), r) for r in range(1, members)], axis=1
    )
    hidden = mine(x).astype(f32) + matmul(normed_heads, w_heads, 1, 1)
    unit_two, factor_two, scaled_two = rms_parts(hidden, norm2_gain)
    normed2 = gather_in_parts(scaled_two, count)
    pre = matmul(normed2, w_gu)
    gate_pre, up_pre = pre[:, :hidden_units], pre[:, hidden_units:]
    gate_sig = jax.nn.sigmoid(gate_pre)
    gate_silu = gate_pre * gate_sig
    hidden_act = (gate_silu * up_pre).astype(bf16)

    grad_feed = owner_first(cotangent)
    grad_act = matmul(grad_feed, w_d)
    grad_gate = (grad_act * up_pre * gate_sig * (1.0 + gate_pre * (1.0 - gate_sig))).astype(bf16)
    grad_up = (grad_act * gate_silu).astype(bf16)
    grad_gu = jnp.concatenate([grad_gate, grad_up], axis=1)
    part_n2 = matmul(grad_gu, w_gu, 1, 1).astype(bf16)
    grad_n2 = to_shards(part_n2)
    begun = lax.ppermute(part_n2[:16, :128], "dp", [(0, 1), (1, 0)])
    normed2, grad_gu, hidden_act = after((normed2, grad_gu, hidden_act), begun)
    rows_wgu, stages_wgu = scatter_rows(matmul(normed2, grad_gu, 0, 0).astype(bf16))
    feed_part = matmul(hidden_act, w_d, 1, 1).astype(bf16)
    rows_wd, stages_wd = scatter_rows(matmul(grad_feed, hidden_act, 0, 0).astype(bf16))
    gain_two_part = jnp.sum(grad_n2 * unit_two, axis=0)
    grad_hidden = mine(grad_feed).astype(f32) + norm_back(unit_two, factor_two, grad_n2 * norm2_gain)
    grad_attn = gather_in_parts(grad_hidden, count)
    feed = to_shards(after(feed_part, grad_n2))
    grad_o = matmul(grad_attn, w_o)
    grad_o, feed = after((grad_o, feed), stages_wgu[:1], stages_wd[:1])
    output = from_shards(hidden + feed)
    grad_q, gk, gv, row_sums, acts, dk, dv, head_part = run_backward(
        qkv, levels, one, aux, key_in, value_in, gain, mixed, probs, scores, mixed_t, blocks_of(grad_o)
    )
    dk_later, dv_later = exchange(dk, dv, coef_out, False, own_end, near_end)
    grad_wo = matmul(grad_attn, normed_o.reshape(rows, heads), 0, 0).astype(bf16)
    dk_later = after(dk_later, stages_wgu, stages_wd, grad_wo, output)
    grad_k, grad_v, grad_logits = run_finish(
        qkv, levels, one, sig, aux, sums, key_in, value_in, key_own, value_own,
        gk, gv, row_sums, acts, dk_later, dv_later,
    )
    decay_rows = lanes(grad_logits, (count, members))
    grad_all = jnp.concatenate(
        [a.reshape(rows, heads) for a in (grad_q, grad_k, grad_v)] + [decay_rows.T], axis=1
    )
    part_n1 = (matmul(grad_all[:, :cut], w_qkv, 1, 1) + matmul(decay_rows, w_dec, 0, 1)).astype(bf16)
    grad_n1 = to_shards(part_n1)
    rows_wo, _ = scatter_rows(grad_wo)
    grad_in = matmul(normed1, after(grad_all, grad_n1), 0, 0).astype(bf16)
    rows_att, _ = scatter_rows(grad_in)
    gain_one_part = jnp.sum(part_n1.astype(f32) * unit_one, axis=0)
    bias_part = lax.dynamic_update_slice_in_dim(
        jnp.zeros_like(decay_bias),
        jnp.sum(grad_logits.astype(f32), axis=1),
        tp_place * SLOTS,
        0,
    )
    small = jnp.concatenate(
        [gain_one_part, gain_two_part, jnp.sum(head_part, axis=(0, 1)), bias_part]
    )
    small = sum_small(small)
    input_grad = grad_hidden + norm_back(mine(unit_one), mine(factor_one), grad_n1 * norm1_gain)
    input_grad = natural(from_shards(input_grad)).astype(f32)
    return (
        natural(output).reshape(count, tokens, width),
        input_grad.reshape(count, tokens, width),
        small[:width],
        small[width : 2 * width],
        small[2 * width : 2 * width + HEAD_DIM],
        small[2 * width + HEAD_DIM :],
        rows_att[:, :heads],
        rows_att[:, heads : 2 * heads],
        rows_att[:, 2 * heads : cut],
        rows_att[:, cut:],
        rows_wo.T,
        rows_wgu[:, :hidden_units],
        rows_wgu[:, hidden_units:],
        rows_wd.T,
    )


def solution(mesh):
    return jax.shard_map(
        per_device,
        mesh=mesh,
        in_specs=(
            P("dp", "ctx", None),
            P("dp", "ctx"),
            P("dp", "ctx", None),
            P(),
            P(),
            P(),
            P(),
            P(("dp", "ctx"), "tp"),
            P(("dp", "ctx"), "tp"),
            P(("dp", "ctx"), "tp"),
            P(("dp", "ctx"), "tp"),
            P("tp", ("dp", "ctx")),
            P(("dp", "ctx"), "tp"),
            P(("dp", "ctx"), "tp"),
            P("tp", ("dp", "ctx")),
        ),
        out_specs=(
            P("dp", "ctx", None),
            P("dp", "ctx", None),
            P(),
            P(),
            P(),
            P(),
            P(("dp", "ctx"), "tp"),
            P(("dp", "ctx"), "tp"),
            P(("dp", "ctx"), "tp"),
            P(("dp", "ctx"), "tp"),
            P("tp", ("dp", "ctx")),
            P(("dp", "ctx"), "tp"),
            P(("dp", "ctx"), "tp"),
            P("tp", ("dp", "ctx")),
        ),
        check_vma=False,
    )
```

```python
import jax
import jax.numpy as jnp
from jax import lax
from jax.experimental import pallas as pl
from jax.experimental.layout import Layout, with_layout_constraint
from jax.experimental.pallas import tpu as pltpu
from jax.sharding import PartitionSpec as P

HEAD_DIM = 512
SLOTS = 64
CHUNK = 32
epsilon = 1e-05
gate_norm = 8.0
f32 = jnp.float32
bf16 = jnp.bfloat16
NEG = -1e30
SCALE = HEAD_DIM**-0.5


def split2(x):
    high = x.astype(bf16)
    return high, (x - high.astype(f32)).astype(bf16)


def dg(a, b, ca, cb):
    return lax.dot_general(a, b, (((ca,), (cb,)), ((), ())), preferred_element_type=f32)


def dot2(a, b, ca, cb):
    high, low = a
    return dg(high, b, ca, cb) + dg(low, b, ca, cb)


def dot2r(a, b, ca, cb):
    high, low = b
    return dg(a, high, ca, cb) + dg(a, low, ca, cb)


def dot3(a, b, ca, cb):
    return dg(a[0], b[0], ca, cb) + (dg(a[0], b[1], ca, cb) + dg(a[1], b[0], ca, cb))


def group_lane(x, index):
    rows, lanes = x.shape
    lane = lax.broadcasted_iota(jnp.int32, (rows, 128), 1)
    at = (lane // CHUNK) * CHUNK + index
    parts = [
        jnp.take_along_axis(x[:, i : i + 128], at, axis=1, mode="promise_in_bounds")
        for i in range(0, lanes, 128)
    ]
    return jnp.concatenate(parts, axis=1)


def chunk_of(rows, lanes):
    return lax.broadcasted_iota(jnp.int32, (rows, lanes), 1) // CHUNK


def pick_rows(array, rows, chunks, first=0):
    lanes = array.shape[1]
    chunk = chunk_of(rows, lanes)
    total = jnp.zeros((rows, lanes), f32)
    for c in range(first, chunks):
        total = jnp.where(chunk == c, array[(c - first) * rows : (c - first + 1) * rows], total)
    return total


def level_refs(levels):
    slots, tokens = levels.shape
    chunk = chunk_of(slots, tokens)
    refs = jnp.zeros_like(levels)
    for c in range(1, tokens // CHUNK):
        refs = jnp.where(chunk == c, levels[:, c * CHUNK - 1 : c * CHUNK], refs)
    return refs


def stack_chunks(array, chunks):
    chunk = chunk_of(*array.shape)
    return jnp.concatenate([jnp.where(chunk == c, array, 0.0) for c in range(1, chunks)], axis=0)


def rows_of(ref):
    return ref[...].reshape(-1, ref.shape[-1])


def store_rows(ref, value):
    ref[...] = value.reshape(ref.shape)


def store_state(ref, key_part, value_part):
    ref[0, :, :HEAD_DIM] = key_part.astype(ref.dtype)
    ref[0, :, HEAD_DIM:] = value_part.astype(ref.dtype)


def aux_rows(tokens):
    chunks = tokens // CHUNK
    base = 2 * CHUNK + chunks
    return base, base + 8


def make_aux(seg, prev_doc):
    count, tokens = seg.shape
    chunks = tokens // CHUNK
    place = jnp.arange(tokens)
    local = place % CHUNK
    grouped = seg.reshape(count, chunks, CHUNK)
    spread = jnp.repeat(grouped.transpose(0, 2, 1), CHUNK, axis=2)
    index = jnp.arange(CHUNK)[:, None]
    same = spread == seg[:, None, :]
    from_j = same & (local[None, :] >= index)[None]
    to_i = same & (local[None, :] <= index)[None]
    ends = jnp.concatenate([jnp.full((count, 1), -5, seg.dtype), grouped[:, :-1, -1]], axis=1)
    before = (ends[:, :, None] == seg[:, None, :]) & (
        place[None, :] < (jnp.arange(chunks) * CHUNK)[:, None]
    )[None]
    after = jnp.repeat(ends, CHUNK, axis=1) == seg
    first = seg == seg[:, :1]
    last = seg == seg[:, -1:]
    bias = jnp.concatenate(
        [from_j, to_i, before, after[:, None], first[:, None], last[:, None]], axis=1
    )
    bias = jnp.where(bias, 0.0, NEG).astype(f32)
    previous = jnp.concatenate([prev_doc[:, None], seg[:, :-1]], axis=1)
    keeps = (previous == seg).astype(f32)[:, None]
    pad = jnp.zeros((count, 4, tokens), f32)
    return jnp.concatenate([bias, keeps, pad], axis=1)


def state_kernel(k_ref, v_ref, ld_ref, one_ref, aux_ref, lev_ref, st_ref, low_ref, end_ref):
    tokens = ld_ref.shape[1]
    base, _ = aux_rows(tokens)
    earlier = lax.broadcasted_iota(jnp.int32, (tokens, tokens), 0)
    later = lax.broadcasted_iota(jnp.int32, (tokens, tokens), 1)
    upper = jnp.where(earlier <= later, 1.0, 0.0).astype(bf16)
    ld = ld_ref[...]
    high, rest = ld.astype(bf16), None
    rest = ld - high.astype(f32)
    mid, low = split2(rest)
    levels = dg(high, upper, 1, 0) + (dg(mid, upper, 1, 0) + dg(low, upper, 1, 0))
    lev_ref[...] = levels
    tail = jnp.exp(levels[:, tokens - 1 : tokens] - levels + aux_ref[0, base + 2 : base + 3, :])
    tail = split2(tail * one_ref[...])
    state_k, state_v = dot2(tail, rows_of(k_ref), 1, 0), dot2(tail, rows_of(v_ref), 1, 0)
    store_state(st_ref, state_k, state_v)
    store_state(low_ref, state_k, state_v)
    end_ref[0] = jnp.broadcast_to(levels[:, tokens - 1 : tokens], (SLOTS, 128))


def forward_kernel(
    q_ref, k_ref, v_ref, lev_ref, one_ref, aux_ref, ki_ref, vi_ref, gain_ref,
    no_ref, mix_ref, p_ref, sc_ref, mt_ref, w_scr, d_scr, wh_scr, wl_scr,
):
    tokens = lev_ref.shape[1]
    chunks = tokens // CHUNK
    base, _ = aux_rows(tokens)
    levels, one = lev_ref[...], one_ref[...]
    q, k, v = rows_of(q_ref), rows_of(k_ref), rows_of(v_ref)
    chunk = chunk_of(SLOTS, tokens)
    kq = dg(k, q, 1, 1)
    d_scr[...] = pick_rows(kq, CHUNK, chunks)

    def inside(j, scores):
        gap = levels - group_lane(levels, j) + aux_ref[0, pl.ds(j, 1), :]
        w = jnp.exp(gap) * group_lane(one, j)
        w_scr[j] = w
        return scores + w * d_scr[pl.ds(j, 1), :]

    scores = lax.fori_loop(0, CHUNK, inside, jnp.zeros_like(levels), unroll=4)
    decay = jnp.exp(levels - level_refs(levels) + aux_ref[0, base : base + 1, :])
    for c in range(1, chunks):
        w = levels[:, c * CHUNK - 1 : c * CHUNK] - levels + aux_ref[0, 2 * CHUNK + c : 2 * CHUNK + c + 1, :]
        wh, wl = split2(jnp.exp(w) * one)
        wh_scr[(c - 1) * SLOTS : c * SLOTS] = wh
        wl_scr[(c - 1) * SLOTS : c * SLOTS] = wl
    wst = (wh_scr[...], wl_scr[...])
    scores += decay * pick_rows(dot3(wst, split2(kq), 1, 0), SLOTS, chunks, 1)
    carried = jnp.exp(levels + aux_ref[0, base + 1 : base + 2, :])
    scores += carried * dot2(split2(ki_ref[0]), q, 1, 1)
    sc_ref[...] = scores
    z = scores * SCALE
    e = jnp.exp(z - jnp.max(z, axis=0, keepdims=True))
    probs = e / jnp.sum(e, axis=0, keepdims=True)
    p_ref[...] = probs

    def mixing(j, carry):
        d_scr[pl.ds(j, 1), :] = jnp.sum(w_scr[j] * probs, axis=0, keepdims=True)
        return carry

    lax.fori_loop(0, CHUNK, mixing, 0, unroll=4)
    row = lax.broadcasted_iota(jnp.int32, (tokens, tokens), 0) // CHUNK
    col = lax.broadcasted_iota(jnp.int32, (tokens, tokens), 1) // CHUNK
    mixed_t = jnp.where(row == col, jnp.concatenate([d_scr[...]] * chunks, axis=0), 0.0)
    mixed_t += dot3(wst, split2(stack_chunks(probs * decay, chunks)), 0, 0)
    mt_ref[0] = mixed_t
    out = dot2(split2(mixed_t), v, 0, 0) + dot3(split2(probs * carried), split2(vi_ref[0]), 0, 0)
    mix_ref[...] = out
    unit = out * lax.rsqrt(jnp.mean(out * out, axis=1, keepdims=True) + epsilon)
    store_rows(no_ref, (unit * gain_ref[...]).astype(bf16))


def backward_kernel(
    q_ref, k_ref, v_ref, lev_ref, one_ref, aux_ref, ki_ref, vi_ref, gain_ref, mix_ref, p_ref, sc_ref, mt_ref, go_ref,
    gq_ref, gk_ref, gv_ref, r_ref, a_ref, d_ref, low_ref, hg_ref, w_scr, d_scr, e_scr, x_scr, wh_scr, wl_scr,
):
    tokens = lev_ref.shape[1]
    chunks = tokens // CHUNK
    base, _ = aux_rows(tokens)
    levels, one, probs = lev_ref[...], one_ref[...], p_ref[...]
    q, k, v = rows_of(q_ref), rows_of(k_ref), rows_of(v_ref)
    out, go = mix_ref[...], rows_of(go_ref).astype(f32)
    factor = lax.rsqrt(jnp.mean(out * out, axis=1, keepdims=True) + epsilon)
    unit = out * factor
    hg_ref[0] = jnp.sum(go * unit, axis=0, keepdims=True)
    go = go * gain_ref[...]
    grad = factor * (go - unit * jnp.mean(go * unit, axis=1, keepdims=True))
    g = split2(grad)
    kin, vin = split2(ki_ref[0]), split2(vi_ref[0])
    gv = dot2r(v, g, 1, 1)
    d_scr[...] = pick_rows(gv, CHUNK, chunks)

    def inside(j, dp):
        gap = levels - group_lane(levels, j) + aux_ref[0, pl.ds(j, 1), :]
        w = jnp.exp(gap) * group_lane(one, j)
        w_scr[j] = w
        return dp + w * d_scr[pl.ds(j, 1), :]

    dp = lax.fori_loop(0, CHUNK, inside, jnp.zeros_like(levels), unroll=4)
    decay = jnp.exp(levels - level_refs(levels) + aux_ref[0, base : base + 1, :])
    for c in range(1, chunks):
        w = levels[:, c * CHUNK - 1 : c * CHUNK] - levels + aux_ref[0, 2 * CHUNK + c : 2 * CHUNK + c + 1, :]
        w = jnp.exp(w)
        x_scr[(c - 1) * SLOTS : c * SLOTS] = w
        wh, wl = split2(w * one)
        wh_scr[(c - 1) * SLOTS : c * SLOTS] = wh
        wl_scr[(c - 1) * SLOTS : c * SLOTS] = wl
    wst = (wh_scr[...], wl_scr[...])
    dp += decay * pick_rows(dot3(wst, split2(gv), 1, 0), SLOTS, chunks, 1)
    carried = jnp.exp(levels + aux_ref[0, base + 1 : base + 2, :])
    dp += carried * dot3(vin, g, 1, 1)
    dz = SCALE * probs * (dp - jnp.sum(probs * dp, axis=0, keepdims=True))
    a_ref[...] = dz * sc_ref[...] + probs * dp

    def mixing(j, carry):
        d_scr[pl.ds(j, 1), :] = jnp.sum(w_scr[j] * dz, axis=0, keepdims=True)
        return carry

    lax.fori_loop(0, CHUNK, mixing, 0, unroll=4)
    row = lax.broadcasted_iota(jnp.int32, (tokens, tokens), 0) // CHUNK
    col = lax.broadcasted_iota(jnp.int32, (tokens, tokens), 1) // CHUNK
    mz_t = jnp.where(row == col, jnp.concatenate([d_scr[...]] * chunks, axis=0), 0.0)
    zst = split2(stack_chunks(dz * decay, chunks))
    pst = split2(stack_chunks(probs * decay, chunks))
    mz_t += dot3(wst, zst, 0, 0)
    mz = split2(mz_t)
    zc, pc = split2(dz * carried), split2(probs * carried)
    store_rows(gq_ref, (dot2(mz, k, 0, 0) + dot3(zc, kin, 0, 0)).astype(bf16))
    gk_ref[...] = dot2(mz, q, 1, 0)
    gv_ref[...] = dot3(split2(mt_ref[0]), g, 1, 0)
    grad_ks, grad_vs = dot2(zc, q, 1, 0), dot3(pc, g, 1, 0)
    store_state(d_ref, grad_ks, grad_vs)
    store_state(low_ref, grad_ks, grad_vs)
    qk = dg(q, k, 1, 1)
    gv_n = dot2(g, v, 1, 1)
    d_scr[...] = pick_rows(qk, CHUNK, chunks)
    e_scr[...] = pick_rows(gv_n, CHUNK, chunks)

    def onward(i, total):
        gap = group_lane(levels, i) - levels + aux_ref[0, pl.ds(CHUNK + i, 1), :]
        term = group_lane(dz, i) * d_scr[pl.ds(i, 1), :] + group_lane(probs, i) * e_scr[pl.ds(i, 1), :]
        return total + jnp.exp(gap) * term

    total = lax.fori_loop(0, CHUNK, onward, jnp.zeros_like(levels), unroll=4)
    cross = dot3(zst, split2(qk), 1, 0) + dot3(pst, split2(gv_n), 1, 0)
    for c in range(1, chunks):
        total += x_scr[(c - 1) * SLOTS : c * SLOTS] * cross[(c - 1) * SLOTS : c * SLOTS]
    r_ref[...] = total


def finish_kernel(
    k_ref, v_ref, lev_ref, one_ref, sig_ref, aux_ref, sums_ref, ki_ref, vi_ref, ks_ref, vs_ref, gk_ref, gv_ref,
    r_ref, a_ref, dk_ref, dv_ref, gko_ref, gvo_ref, gl_ref,
):
    tokens = lev_ref.shape[1]
    base, _ = aux_rows(tokens)
    levels, one = lev_ref[...], one_ref[...]
    k, v = rows_of(k_ref), rows_of(v_ref)
    tail = jnp.exp(levels[:, tokens - 1 : tokens] - levels + aux_ref[0, base + 2 : base + 3, :])
    end = jnp.exp(levels[:, tokens - 1 : tokens] + aux_ref[0, base + 1 : base + 2, tokens - 1 : tokens])
    dk, dv = dk_ref[0], dv_ref[0]
    dks, dvs = split2(dk), split2(dv)
    weights = split2(tail * one)
    store_rows(gko_ref, (gk_ref[...] + dot3(weights, dks, 0, 0)).astype(bf16))
    store_rows(gvo_ref, (gv_ref[...] + dot3(weights, dvs, 0, 0)).astype(bf16))
    rows = r_ref[...] + tail * (dot2(dks, k, 1, 1) + dot2(dvs, v, 1, 1))
    final_k = end * ki_ref[0] + ks_ref[0]
    final_v = end * vi_ref[0] + vs_ref[0]
    at_end = jnp.sum(dk * final_k + dv * final_v, axis=1, keepdims=True)
    x = a_ref[...] - one * rows
    high = x.astype(bf16)
    mid, low = split2(x - high.astype(f32))
    sums = sums_ref[0]
    flow = dg(high, sums, 1, 0) + (dg(mid, sums, 1, 0) + dg(low, sums, 1, 0))
    flow += jnp.where(aux_ref[0, base + 2 : base + 3, :] == 0.0, at_end, 0.0)
    grad = flow * aux_ref[0, base + 3 : base + 4, :] - (1.0 - one) * rows
    gl_ref[...] = (grad * sig_ref[...]).astype(bf16)


def seq_specs(tokens, members):
    def own(col):
        return pl.BlockSpec((members, 1, tokens // members, HEAD_DIM), lambda i: (0, i, 0, col))

    tok = pl.BlockSpec((tokens, HEAD_DIM), lambda i: (i, 0))
    lane = pl.BlockSpec((SLOTS, tokens), lambda i: (0, i))
    _, rows = aux_rows(tokens)
    aux = pl.BlockSpec((1, rows, tokens), lambda i: (i, 0, 0))
    state = pl.BlockSpec((1, SLOTS, 2 * HEAD_DIM), lambda i: (i, 0, 0))
    key_half = pl.BlockSpec((1, SLOTS, HEAD_DIM), lambda i: (i, 0, 0))
    value_half = pl.BlockSpec((1, SLOTS, HEAD_DIM), lambda i: (i, 0, 1))
    halves = [key_half, value_half]
    gain = pl.BlockSpec((1, HEAD_DIM), lambda i: (0, 0))
    square = pl.BlockSpec((1, tokens, tokens), lambda i: (i, 0, 0))
    row = pl.BlockSpec((1, 1, HEAD_DIM), lambda i: (i, 0, 0))
    return own, tok, lane, aux, state, halves, gain, square, row


def params(mib):
    return pltpu.CompilerParams(vmem_limit_bytes=mib << 20)


def cost(count, flops, size):
    return pl.CostEstimate(flops=count * flops, bytes_accessed=count * size, transcendentals=count * 1000000)


def shape(dims, dtype):
    return jax.ShapeDtypeStruct(dims, dtype)


def run_states(qkv, ld, one, aux):
    count, _, tokens = aux.shape
    own, tok, lane, auxs, state, _, _, _, _ = seq_specs(tokens, qkv.shape[0])
    return pl.pallas_call(
        state_kernel,
        grid=(count,),
        in_specs=[own(1), own(2), lane, lane, auxs],
        out_specs=[lane, state, state, pl.BlockSpec((1, SLOTS, 128), lambda i: (i, 0, 0))],
        out_shape=[
            shape((SLOTS, count * tokens), f32),
            shape((count, SLOTS, 2 * HEAD_DIM), f32),
            shape((count, SLOTS, 2 * HEAD_DIM), bf16),
            shape((count, SLOTS, 128), f32),
        ],
        compiler_params=params(24),
        cost_estimate=cost(count, 100000000, 1500000),
    )(qkv, qkv, ld, one, aux)


def big_scratch(tokens):
    stack = (tokens // CHUNK - 1) * SLOTS
    return stack


def run_forward(qkv, levels, one, aux, state_in, gain):
    count, _, tokens = aux.shape
    own, tok, lane, auxs, state, halves, gains, square, _ = seq_specs(tokens, qkv.shape[0])
    stack = big_scratch(tokens)
    return pl.pallas_call(
        forward_kernel,
        grid=(count,),
        in_specs=[own(0), own(1), own(2), lane, lane, auxs, *halves, gains],
        out_specs=[own(0), tok, lane, lane, square],
        out_shape=[
            shape(qkv.shape[:3] + (HEAD_DIM,), bf16),
            shape((count * tokens, HEAD_DIM), f32),
            shape((SLOTS, count * tokens), f32),
            shape((SLOTS, count * tokens), f32),
            shape((count, tokens, tokens), f32),
        ],
        scratch_shapes=[
            pltpu.VMEM((CHUNK, SLOTS, tokens), f32),
            pltpu.VMEM((CHUNK, tokens), f32),
            pltpu.VMEM((stack, tokens), bf16),
            pltpu.VMEM((stack, tokens), bf16),
        ],
        compiler_params=params(40),
        cost_estimate=cost(count, 1000000000, 3000000),
    )(qkv, qkv, qkv, levels, one, aux, state_in, state_in, gain)


def run_backward(qkv, levels, one, aux, state_in, gain, mixed, probs, scores, mixed_t, grad_o):
    count, _, tokens = aux.shape
    own, tok, lane, auxs, state, halves, gains, square, row = seq_specs(tokens, qkv.shape[0])
    stack = big_scratch(tokens)
    return pl.pallas_call(
        backward_kernel,
        grid=(count,),
        in_specs=[own(0), own(1), own(2), lane, lane, auxs, *halves, gains, tok, lane, lane, square, own(0)],
        out_specs=[own(0), tok, tok, lane, lane, state, state, row],
        out_shape=[
            shape(qkv.shape[:3] + (HEAD_DIM,), bf16),
            shape((count * tokens, HEAD_DIM), f32),
            shape((count * tokens, HEAD_DIM), f32),
            shape((SLOTS, count * tokens), f32),
            shape((SLOTS, count * tokens), f32),
            shape((count, SLOTS, 2 * HEAD_DIM), f32),
            shape((count, SLOTS, 2 * HEAD_DIM), bf16),
            shape((count, 1, HEAD_DIM), f32),
        ],
        scratch_shapes=[
            pltpu.VMEM((CHUNK, SLOTS, tokens), f32),
            pltpu.VMEM((CHUNK, tokens), f32),
            pltpu.VMEM((CHUNK, tokens), f32),
            pltpu.VMEM((stack, tokens), f32),
            pltpu.VMEM((stack, tokens), bf16),
            pltpu.VMEM((stack, tokens), bf16),
        ],
        compiler_params=params(48),
        cost_estimate=cost(count, 3000000000, 5000000),
    )(qkv, qkv, qkv, levels, one, aux, state_in, state_in, gain, mixed, probs, scores, mixed_t, grad_o)


def run_finish(qkv, levels, one, sig, aux, sums, state_in, state_own, gk, gv, rows, acts, grad_later):
    count, _, tokens = aux.shape
    own, tok, lane, auxs, state, halves, _, square, _ = seq_specs(tokens, qkv.shape[0])
    return pl.pallas_call(
        finish_kernel,
        grid=(count,),
        in_specs=[own(1), own(2), lane, lane, lane, auxs, square, *halves, *halves]
        + [tok, tok, lane, lane, *halves],
        out_specs=[own(0), own(0), lane],
        out_shape=[
            shape(qkv.shape[:3] + (HEAD_DIM,), bf16),
            shape(qkv.shape[:3] + (HEAD_DIM,), bf16),
            shape((SLOTS, count * tokens), bf16),
        ],
        compiler_params=params(40),
        cost_estimate=cost(count, 300000000, 4000000),
    )(
        qkv, qkv, levels, one, sig, aux, sums, state_in, state_in, state_own, state_own,
        gk, gv, rows, acts, grad_later, grad_later,
    )


def matmul(a, b, ca=1, cb=0):
    return lax.dot_general(a, b, (((ca,), (cb,)), ((), ())), preferred_element_type=f32)


def rms_parts(array, gain_vec):
    factor = lax.rsqrt(jnp.mean(array * array, axis=-1, keepdims=True) + epsilon)
    unit_val = array * factor
    return unit_val, factor, unit_val * gain_vec


def norm_back(unit_val, factor, grad_unit):
    return factor * (grad_unit - unit_val * jnp.mean(grad_unit * unit_val, axis=-1, keepdims=True))


def row_major(array):
    return with_layout_constraint(array, Layout(major_to_minor=tuple(range(array.ndim))))


def tie(*values):
    return lax.optimization_barrier(values)


def line_gather(parts, axis, buffer):
    size, here = lax.axis_size(axis), lax.axis_index(axis)
    count = parts.shape[0]
    moving = {to: [parts[c] for c in range(count)] for to in (1, -1)}
    for s in range(1, size):
        for c in range(count):
            for to in (1, -1):
                sources = range(s - 1, size - 1) if to == 1 else range(1, size - s + 1)
                value = lax.ppermute(moving[to][c], axis, [(i, i + to) for i in sources])
                moving[to][c] = value
                origin = here - s * to
                valid = (origin >= 0) & (origin < size)
                at = (jnp.where(valid, origin, here), c) + (0,) * (parts.ndim - 1)
                buffer = lax.dynamic_update_slice(buffer, value[None, None], at)
    return lax.dynamic_update_slice(buffer, parts[None], (here,) + (0,) * parts.ndim)


def per_device(
    layer_input, segments, cotangent, norm1_gain, norm2_gain, head_gain, decay_bias,
    w_query, w_key, w_value, w_decay, w_out, w_gate, w_up, w_down,
):
    count, tokens, width = layer_input.shape
    rows = count * tokens
    hidden_units = w_gate.shape[1]
    heads = w_query.shape[1]
    tp_place, here = lax.axis_index("tp"), lax.axis_index("ctx")
    swap_x = [(0, 1), (1, 0), (2, 3), (3, 2)]
    places, members = lax.axis_size("ctx"), lax.axis_size("tp")
    part = tokens // members

    def owner_first(array):
        array = array.reshape(count, members, part, width).transpose(1, 0, 2, 3)
        return array.reshape(rows, width)

    def natural(array):
        return array.reshape(members, count, part, width).transpose(1, 0, 2, 3)

    def lanes(array, order):
        array = array.reshape(array.shape[0], *order, part).transpose(0, 2, 1, 3)
        return array.reshape(array.shape[0], rows)

    def blocks_of(array):
        return array.reshape(members, count, part, -1)

    def mine(array):
        return lax.dynamic_slice_in_dim(array, tp_place * (count * part), count * part, 0)

    def to_shards(array):
        return lax.psum_scatter(array, "tp", scatter_dimension=0, tiled=True)

    def from_shards(array):
        return lax.all_gather(array.astype(bf16), "tp", axis=0, tiled=True)

    def gather_rows(array):
        return lax.all_gather(array, ("dp", "ctx"), axis=0, tiled=True)

    core, y, x_at = lax.axis_index("dp"), here // 2, here % 2
    swap_y = [(0, 2), (2, 0), (1, 3), (3, 1)]

    def pick(value, index, axis):
        return lax.dynamic_index_in_dim(value, index, axis, keepdims=False)

    def add(a, b, dtype=bf16):
        return row_major((a.astype(f32) + b.astype(f32)).astype(dtype))

    def scatter_cores(array):
        if places != 4:
            return (array,)
        array = row_major(array).reshape(2, 2, 2, array.shape[0] // 8, array.shape[1])
        other = lax.ppermute(pick(array, 1 - core, 0), "dp", [(0, 1), (1, 0)])
        return pick(array, core, 0), other

    def scatter_first(held):
        if places != 4:
            return held
        chip = add(*held)
        half = chip.shape[2] // 2
        upper, lower = chip[:, :, :half], chip[:, :, half:]
        return (
            pick(upper, x_at, 1),
            pick(lower, y, 0),
            lax.ppermute(pick(upper, 1 - x_at, 1), "ctx", swap_x),
            lax.ppermute(pick(lower, 1 - y, 0), "ctx", swap_y),
        )

    def scatter_second(held):
        if places != 4:
            return held
        upper, lower, over_x, over_y = held
        upper, lower = add(upper, over_x), add(lower, over_y)
        return (
            pick(upper, y, 0),
            pick(lower, x_at, 0),
            lax.ppermute(pick(upper, 1 - y, 0), "ctx", swap_y),
            lax.ppermute(pick(lower, 1 - x_at, 0), "ctx", swap_x),
        )

    def scatter_end(held):
        if places != 4:
            return lax.psum_scatter(
                held[0], ("dp", "ctx"), scatter_dimension=0, tiled=True
            ).astype(f32)
        upper, lower, over_y, over_x = held
        return row_major(jnp.concatenate([add(upper, over_y, f32), add(lower, over_x, f32)], axis=0))

    def gather_in_parts(array, parts):
        buffer = jnp.zeros((members, parts, count * part // parts, width), bf16)
        return line_gather(array.astype(bf16).reshape(buffer.shape[1:]), "tp", buffer).reshape(rows, width)

    def from_partner(array, distance):
        return lax.ppermute(array, "tp", [(i, i ^ distance) for i in range(members)])

    cut = 3 * heads
    w_in = gather_rows(jnp.concatenate([w_query, w_key, w_value, w_decay], axis=1))
    w_qkv, w_dec = w_in[:, :cut], w_in[:, cut:]
    w_out_t = w_out.T
    w_heads = gather_rows(
        jnp.concatenate([w_out_t] + [from_partner(w_out_t, r) for r in range(1, members)], axis=1)
    )
    w_rest = gather_rows(jnp.concatenate([w_gate, w_up, w_down.T], axis=1))
    w_gu = w_rest[:, : 2 * hidden_units]
    w_d = w_rest[:, 2 * hidden_units :]

    edges = lax.all_gather(jnp.stack([segments[:, 0], segments[:, -1]]), "ctx")
    prev_doc = jnp.where(here > 0, edges[jnp.maximum(here - 1, 0), 1], -1)
    aux = make_aux(segments, prev_doc)
    place = jnp.arange(tokens)
    sums = (
        (place[:, None] >= place[None, :])[None] & (segments[:, :, None] == segments[:, None, :])
    ).astype(bf16)
    index = jnp.arange(places)
    reach_in = (index[:, None] < here) & (edges[:, 1] == segments[:, 0])
    reach_out = (index[:, None] > here) & (edges[:, 0] == segments[:, -1])

    def flag(array):
        return array.astype(f32)[:, None, None]

    if places == 4:
        beside = here ^ 1
        is_low = x_at == 0

        def level_ends(own_end):
            return lax.ppermute(own_end, "ctx", swap_x)

        def exchange(own, low, forward, own_end, near_end):
            row = lax.dynamic_slice_in_dim(edges, 2 * y, 2, 0)
            if forward:
                reach, pairs, origin, side = reach_in, [(0, 2), (1, 3)], 1, 1
                through = jnp.where(is_low, near_end, own_end)
            else:
                reach, pairs, origin, side = reach_out, [(2, 0), (3, 1)], 2, 0
                through = jnp.where(is_low, own_end, near_end)
            near = lax.ppermute(low, "ctx", swap_x).astype(f32)
            keeps = flag(row[0, side] == row[1, side])
            keeps = (keeps * jnp.exp(through))[..., :1]
            outer = is_low if forward else ~is_low
            joined = jnp.where(outer, near + keeps * own, own + keeps * near)
            far = lax.ppermute(joined.astype(bf16), "ctx", pairs).astype(f32)
            distant = ~is_low if forward else is_low
            scale = jnp.where(distant, jnp.exp(near_end), 1.0)[..., :1]
            near_flag = flag(lax.dynamic_index_in_dim(reach, beside, 0, False))
            return near_flag * near + (flag(reach[origin]) * scale) * far

    else:
        between = (index[None, :] > jnp.minimum(index[:, None], here)) & (
            index[None, :] < jnp.maximum(index[:, None], here)
        )

        def level_ends(own_end):
            return own_end

        def exchange(own, low, forward, own_end, near_end):
            ends = lax.all_gather(own_end[..., :1], "ctx")
            span = jnp.where(between[:, :, None, None, None], ends[None], 0.0)
            span = jnp.exp(jnp.sum(span, axis=1))
            coefs = jnp.where((reach_in if forward else reach_out)[..., None, None], span, 0.0)
            return jnp.sum(lax.all_gather(own, "ctx") * coefs, axis=0)

    x = owner_first(layer_input)
    unit_one, factor_one, scaled_one = rms_parts(x.astype(f32), norm1_gain)
    normed1 = scaled_one.astype(bf16)
    qkv = blocks_of(matmul(normed1, w_qkv).astype(bf16))
    bias_here = lax.dynamic_slice_in_dim(decay_bias, tp_place * SLOTS, SLOTS)
    logits = lanes(matmul(w_dec, normed1, 0, 1), (members, count)) + bias_here[:, None]
    log_decay = jax.nn.log_sigmoid(logits) / gate_norm
    one = -jnp.expm1(log_decay)
    sig = jax.nn.sigmoid(-logits) / gate_norm
    levels, state_own, state_low, own_end = run_states(qkv, log_decay, one, aux)
    near_end = level_ends(own_end)
    state_in = exchange(state_own, state_low, True, own_end, near_end)
    gain = head_gain[None, :]
    normed_o, mixed, probs, scores, mixed_t = run_forward(qkv, levels, one, aux, state_in, gain)
    by_owner = normed_o.reshape(members, count * part, heads)

    def for_partner(r):
        return lax.dynamic_index_in_dim(by_owner, tp_place ^ r, 0, keepdims=False)

    normed_heads = jnp.concatenate(
        [for_partner(0)] + [from_partner(for_partner(r), r) for r in range(1, members)], axis=1
    )
    hidden = mine(x).astype(f32) + matmul(normed_heads, w_heads, 1, 1)
    unit_two, factor_two, scaled_two = rms_parts(hidden, norm2_gain)
    normed2 = gather_in_parts(scaled_two, count)
    pre = matmul(normed2, w_gu)
    gate_pre, up_pre = pre[:, :hidden_units], pre[:, hidden_units:]
    gate_sig = jax.nn.sigmoid(gate_pre)
    gate_silu = gate_pre * gate_sig
    hidden_act = (gate_silu * up_pre).astype(bf16)

    grad_feed = owner_first(cotangent)
    grad_act = matmul(grad_feed, w_d)
    grad_gate = (grad_act * up_pre * gate_sig * (1.0 + gate_pre * (1.0 - gate_sig))).astype(bf16)
    grad_up = (grad_act * gate_silu).astype(bf16)
    grad_gu = jnp.concatenate([grad_gate, grad_up], axis=1)
    part_n2 = matmul(grad_gu, w_gu, 1, 1).astype(bf16)
    grad_n2 = to_shards(part_n2).astype(f32)
    held_wgu = scatter_cores(matmul(normed2, grad_gu, 0, 0).astype(bf16))
    held_wd = scatter_cores(matmul(grad_feed, hidden_act, 0, 0).astype(bf16))
    feed_part = matmul(hidden_act, w_d, 1, 1).astype(bf16)
    gain_two_part = jnp.sum(grad_n2 * unit_two, axis=0)
    grad_hidden = mine(grad_feed).astype(f32) + norm_back(unit_two, factor_two, grad_n2 * norm2_gain)
    grad_attn = grad_hidden.astype(bf16)
    sent = matmul(grad_attn, w_heads).astype(bf16)
    sent, held_wgu, held_wd = tie(sent, held_wgu, held_wd)
    feed = to_shards(feed_part)
    arrived = [sent[:, :heads]] + [
        from_partner(sent[:, r * heads : (r + 1) * heads], r) for r in range(1, members)
    ]
    held_wgu, held_wd = scatter_first(held_wgu), scatter_first(held_wd)
    grad_o = jnp.zeros((members, count * part, heads), bf16)
    for r in range(members):
        grad_o = lax.dynamic_update_slice(grad_o, arrived[r][None], (tp_place ^ r, 0, 0))
    grad_q, gk, gv, row_sums, acts, grad_state, grad_low, head_part = run_backward(
        qkv, levels, one, aux, state_in, gain, mixed, probs, scores, mixed_t, blocks_of(grad_o)
    )
    grad_low, feed, held_wgu, grad_attn = tie(grad_low, feed, held_wgu, grad_attn)
    out_shard = (hidden + feed.astype(f32)).astype(bf16)
    grad_low, out_shard = tie(grad_low, out_shard)
    output = from_shards(out_shard)
    grad_later = exchange(grad_state, grad_low, False, own_end, near_end)
    grad_k, grad_v, grad_logits = run_finish(
        qkv, levels, one, sig, aux, sums, state_in, state_own, gk, gv, row_sums, acts, grad_later
    )
    decay_rows = lanes(grad_logits, (count, members))
    grad_all = jnp.concatenate(
        [a.reshape(rows, heads) for a in (grad_q, grad_k, grad_v)] + [decay_rows.T], axis=1
    )
    part_n1 = (matmul(grad_all[:, :cut], w_qkv, 1, 1) + matmul(decay_rows, w_dec, 0, 1)).astype(bf16)
    part_n1, output, grad_all = tie(part_n1, output, grad_all)
    grad_n1 = to_shards(part_n1)
    gain_one_part = jnp.sum(part_n1.astype(f32) * unit_one, axis=0)
    bias_part = lax.dynamic_update_slice_in_dim(
        jnp.zeros_like(decay_bias),
        jnp.sum(grad_logits.astype(f32), axis=1),
        tp_place * SLOTS,
        0,
    )
    small = jnp.concatenate(
        [gain_one_part, gain_two_part, jnp.sum(head_part, axis=(0, 1)), bias_part]
    )
    held_wo = scatter_first(scatter_cores(matmul(grad_attn, normed_heads, 0, 0).astype(bf16)))
    grad_in = matmul(normed1, grad_all, 0, 0).astype(bf16)
    held_in = scatter_cores(grad_in)
    grad_n1, small, held_in, held_wd = tie(grad_n1, small, held_in, held_wd)
    held_wgu, held_wo = scatter_second(held_wgu), scatter_second(held_wo)
    input_grad = grad_hidden + norm_back(mine(unit_one), mine(factor_one), grad_n1.astype(f32) * norm1_gain)
    input_grad = from_shards(input_grad)
    held_wd = scatter_second(held_wd)
    if places != 4:
        small = lax.psum(small, ("dp", "ctx", "tp"))
    else:
        small += lax.ppermute(small, "dp", [(0, 1), (1, 0)])
        for axis in ("ctx", "tp"):
            for r in (1, 2):
                small += lax.ppermute(small, axis, [(i, i ^ r) for i in range(4)])
    held_in = scatter_first(held_in)
    rows_wo, rows_wgu, rows_wd = scatter_end(held_wo), scatter_end(held_wgu), scatter_end(held_wd)
    rows_att = scatter_end(scatter_second(held_in))
    rows_wo = rows_wo[:, :heads] + sum(
        from_partner(rows_wo[:, r * heads : (r + 1) * heads].astype(bf16), r).astype(f32)
        for r in range(1, members)
    )
    input_grad = natural(input_grad).astype(f32)
    return (
        natural(output).reshape(count, tokens, width),
        input_grad.reshape(count, tokens, width),
        small[:width],
        small[width : 2 * width],
        small[2 * width : 2 * width + HEAD_DIM],
        small[2 * width + HEAD_DIM :],
        rows_att[:, :heads],
        rows_att[:, heads : 2 * heads],
        rows_att[:, 2 * heads : cut],
        rows_att[:, cut:],
        rows_wo.T,
        rows_wgu[:, :hidden_units],
        rows_wgu[:, hidden_units:],
        rows_wd.T,
    )


def solution(mesh):
    return jax.shard_map(
        per_device,
        mesh=mesh,
        in_specs=(
            P("dp", "ctx", None),
            P("dp", "ctx"),
            P("dp", "ctx", None),
            P(),
            P(),
            P(),
            P(),
            P(("dp", "ctx"), "tp"),
            P(("dp", "ctx"), "tp"),
            P(("dp", "ctx"), "tp"),
            P(("dp", "ctx"), "tp"),
            P("tp", ("dp", "ctx")),
            P(("dp", "ctx"), "tp"),
            P(("dp", "ctx"), "tp"),
            P("tp", ("dp", "ctx")),
        ),
        out_specs=(
            P("dp", "ctx", None),
            P("dp", "ctx", None),
            P(),
            P(),
            P(),
            P(),
            P(("dp", "ctx"), "tp"),
            P(("dp", "ctx"), "tp"),
            P(("dp", "ctx"), "tp"),
            P(("dp", "ctx"), "tp"),
            P("tp", ("dp", "ctx")),
            P(("dp", "ctx"), "tp"),
            P(("dp", "ctx"), "tp"),
            P("tp", ("dp", "ctx")),
        ),
        check_vma=False,
    )
```

```python
import jax
import jax.numpy as jnp
from jax import lax
from jax.experimental import pallas as pl
from jax.experimental.layout import Layout, with_layout_constraint
from jax.experimental.pallas import tpu as pltpu
from jax.sharding import PartitionSpec as P

HEAD_DIM = 512
SLOTS = 64
CHUNK = 32
epsilon = 1e-05
gate_norm = 8.0
f32 = jnp.float32
bf16 = jnp.bfloat16
NEG = -1e30
SCALE = HEAD_DIM**-0.5


def split2(x):
    high = x.astype(bf16)
    return high, (x - high.astype(f32)).astype(bf16)


def dg(a, b, ca, cb):
    return lax.dot_general(a, b, (((ca,), (cb,)), ((), ())), preferred_element_type=f32)


def dot2(a, b, ca, cb):
    high, low = a
    return dg(high, b, ca, cb) + dg(low, b, ca, cb)


def dot2r(a, b, ca, cb):
    high, low = b
    return dg(a, high, ca, cb) + dg(a, low, ca, cb)


def dot3(a, b, ca, cb):
    return dg(a[0], b[0], ca, cb) + (dg(a[0], b[1], ca, cb) + dg(a[1], b[0], ca, cb))


def group_lane(x, index):
    rows, lanes = x.shape
    lane = lax.broadcasted_iota(jnp.int32, (rows, 128), 1)
    at = (lane // CHUNK) * CHUNK + index
    parts = [
        jnp.take_along_axis(x[:, i : i + 128], at, axis=1, mode="promise_in_bounds")
        for i in range(0, lanes, 128)
    ]
    return jnp.concatenate(parts, axis=1)


def chunk_of(rows, lanes):
    return lax.broadcasted_iota(jnp.int32, (rows, lanes), 1) // CHUNK


def pick_rows(array, rows, chunks, first=0):
    lanes = array.shape[1]
    chunk = chunk_of(rows, lanes)
    total = jnp.zeros((rows, lanes), f32)
    for c in range(first, chunks):
        total = jnp.where(chunk == c, array[(c - first) * rows : (c - first + 1) * rows], total)
    return total


def level_refs(levels):
    slots, tokens = levels.shape
    chunk = chunk_of(slots, tokens)
    refs = jnp.zeros_like(levels)
    for c in range(1, tokens // CHUNK):
        refs = jnp.where(chunk == c, levels[:, c * CHUNK - 1 : c * CHUNK], refs)
    return refs


def stack_chunks(array, chunks):
    chunk = chunk_of(*array.shape)
    return jnp.concatenate([jnp.where(chunk == c, array, 0.0) for c in range(1, chunks)], axis=0)


def rows_of(ref):
    return ref[...].reshape(-1, ref.shape[-1])


def store_rows(ref, value):
    ref[...] = value.reshape(ref.shape)


def store_state(ref, key_part, value_part):
    ref[0, :, :HEAD_DIM] = key_part.astype(ref.dtype)
    ref[0, :, HEAD_DIM:] = value_part.astype(ref.dtype)


def aux_rows(tokens):
    chunks = tokens // CHUNK
    base = 2 * CHUNK + chunks
    return base, base + 8


def make_aux(seg, prev_doc):
    count, tokens = seg.shape
    chunks = tokens // CHUNK
    place = jnp.arange(tokens)
    local = place % CHUNK
    grouped = seg.reshape(count, chunks, CHUNK)
    spread = jnp.repeat(grouped.transpose(0, 2, 1), CHUNK, axis=2)
    index = jnp.arange(CHUNK)[:, None]
    same = spread == seg[:, None, :]
    from_j = same & (local[None, :] >= index)[None]
    to_i = same & (local[None, :] <= index)[None]
    ends = jnp.concatenate([jnp.full((count, 1), -5, seg.dtype), grouped[:, :-1, -1]], axis=1)
    before = (ends[:, :, None] == seg[:, None, :]) & (
        place[None, :] < (jnp.arange(chunks) * CHUNK)[:, None]
    )[None]
    after = jnp.repeat(ends, CHUNK, axis=1) == seg
    first = seg == seg[:, :1]
    last = seg == seg[:, -1:]
    bias = jnp.concatenate(
        [from_j, to_i, before, after[:, None], first[:, None], last[:, None]], axis=1
    )
    bias = jnp.where(bias, 0.0, NEG).astype(f32)
    previous = jnp.concatenate([prev_doc[:, None], seg[:, :-1]], axis=1)
    keeps = (previous == seg).astype(f32)[:, None]
    pad = jnp.zeros((count, 4, tokens), f32)
    return jnp.concatenate([bias, keeps, pad], axis=1)


def state_kernel(k_ref, v_ref, ld_ref, one_ref, aux_ref, lev_ref, st_ref, low_ref, end_ref):
    tokens = ld_ref.shape[1]
    base, _ = aux_rows(tokens)
    earlier = lax.broadcasted_iota(jnp.int32, (tokens, tokens), 0)
    later = lax.broadcasted_iota(jnp.int32, (tokens, tokens), 1)
    upper = jnp.where(earlier <= later, 1.0, 0.0).astype(bf16)
    ld = ld_ref[...]
    high, rest = ld.astype(bf16), None
    rest = ld - high.astype(f32)
    mid, low = split2(rest)
    levels = dg(high, upper, 1, 0) + (dg(mid, upper, 1, 0) + dg(low, upper, 1, 0))
    lev_ref[...] = levels
    tail = jnp.exp(levels[:, tokens - 1 : tokens] - levels + aux_ref[0, base + 2 : base + 3, :])
    tail = split2(tail * one_ref[...])
    state_k, state_v = dot2(tail, rows_of(k_ref), 1, 0), dot2(tail, rows_of(v_ref), 1, 0)
    store_state(st_ref, state_k, state_v)
    store_state(low_ref, state_k, state_v)
    end_ref[0] = jnp.broadcast_to(levels[:, tokens - 1 : tokens], (SLOTS, 128))


def forward_kernel(
    q_ref, k_ref, v_ref, lev_ref, one_ref, aux_ref, ki_ref, vi_ref, gain_ref,
    no_ref, mix_ref, p_ref, sc_ref, mt_ref, w_scr, d_scr, wh_scr, wl_scr,
):
    tokens = lev_ref.shape[1]
    chunks = tokens // CHUNK
    base, _ = aux_rows(tokens)
    levels, one = lev_ref[...], one_ref[...]
    q, k, v = rows_of(q_ref), rows_of(k_ref), rows_of(v_ref)
    chunk = chunk_of(SLOTS, tokens)
    kq = dg(k, q, 1, 1)
    d_scr[...] = pick_rows(kq, CHUNK, chunks)

    def inside(j, scores):
        gap = levels - group_lane(levels, j) + aux_ref[0, pl.ds(j, 1), :]
        w = jnp.exp(gap) * group_lane(one, j)
        w_scr[j] = w
        return scores + w * d_scr[pl.ds(j, 1), :]

    scores = lax.fori_loop(0, CHUNK, inside, jnp.zeros_like(levels), unroll=8)
    decay = jnp.exp(levels - level_refs(levels) + aux_ref[0, base : base + 1, :])
    for c in range(1, chunks):
        w = levels[:, c * CHUNK - 1 : c * CHUNK] - levels + aux_ref[0, 2 * CHUNK + c : 2 * CHUNK + c + 1, :]
        wh, wl = split2(jnp.exp(w) * one)
        wh_scr[(c - 1) * SLOTS : c * SLOTS] = wh
        wl_scr[(c - 1) * SLOTS : c * SLOTS] = wl
    wst = (wh_scr[...], wl_scr[...])
    scores += decay * pick_rows(dot3(wst, split2(kq), 1, 0), SLOTS, chunks, 1)
    carried = jnp.exp(levels + aux_ref[0, base + 1 : base + 2, :])
    scores += carried * dot2(split2(ki_ref[0]), q, 1, 1)
    sc_ref[...] = scores
    z = scores * SCALE
    e = jnp.exp(z - jnp.max(z, axis=0, keepdims=True))
    probs = e / jnp.sum(e, axis=0, keepdims=True)
    p_ref[...] = probs

    def mixing(j, carry):
        d_scr[pl.ds(j, 1), :] = jnp.sum(w_scr[j] * probs, axis=0, keepdims=True)
        return carry

    lax.fori_loop(0, CHUNK, mixing, 0, unroll=8)
    row = lax.broadcasted_iota(jnp.int32, (tokens, tokens), 0) // CHUNK
    col = lax.broadcasted_iota(jnp.int32, (tokens, tokens), 1) // CHUNK
    mixed_t = jnp.where(row == col, jnp.concatenate([d_scr[...]] * chunks, axis=0), 0.0)
    mixed_t += dot3(wst, split2(stack_chunks(probs * decay, chunks)), 0, 0)
    mt_ref[0] = mixed_t
    out = dot2(split2(mixed_t), v, 0, 0) + dot3(split2(probs * carried), split2(vi_ref[0]), 0, 0)
    mix_ref[...] = out
    unit = out * lax.rsqrt(jnp.mean(out * out, axis=1, keepdims=True) + epsilon)
    store_rows(no_ref, (unit * gain_ref[...]).astype(bf16))


def backward_kernel(
    q_ref, k_ref, v_ref, lev_ref, one_ref, aux_ref, ki_ref, vi_ref, gain_ref, mix_ref, p_ref, sc_ref, mt_ref, go_ref,
    gq_ref, gk_ref, gv_ref, r_ref, a_ref, d_ref, low_ref, hg_ref, w_scr, d_scr, e_scr, x_scr, wh_scr, wl_scr,
):
    tokens = lev_ref.shape[1]
    chunks = tokens // CHUNK
    base, _ = aux_rows(tokens)
    levels, one, probs = lev_ref[...], one_ref[...], p_ref[...]
    q, k, v = rows_of(q_ref), rows_of(k_ref), rows_of(v_ref)
    out, go = mix_ref[...], rows_of(go_ref).astype(f32)
    factor = lax.rsqrt(jnp.mean(out * out, axis=1, keepdims=True) + epsilon)
    unit = out * factor
    hg_ref[0] = jnp.sum(go * unit, axis=0, keepdims=True)
    go = go * gain_ref[...]
    grad = factor * (go - unit * jnp.mean(go * unit, axis=1, keepdims=True))
    g = split2(grad)
    kin, vin = split2(ki_ref[0]), split2(vi_ref[0])
    gv = dot2r(v, g, 1, 1)
    d_scr[...] = pick_rows(gv, CHUNK, chunks)

    def inside(j, dp):
        gap = levels - group_lane(levels, j) + aux_ref[0, pl.ds(j, 1), :]
        w = jnp.exp(gap) * group_lane(one, j)
        w_scr[j] = w
        return dp + w * d_scr[pl.ds(j, 1), :]

    dp = lax.fori_loop(0, CHUNK, inside, jnp.zeros_like(levels), unroll=8)
    decay = jnp.exp(levels - level_refs(levels) + aux_ref[0, base : base + 1, :])
    for c in range(1, chunks):
        w = levels[:, c * CHUNK - 1 : c * CHUNK] - levels + aux_ref[0, 2 * CHUNK + c : 2 * CHUNK + c + 1, :]
        w = jnp.exp(w)
        x_scr[(c - 1) * SLOTS : c * SLOTS] = w
        wh, wl = split2(w * one)
        wh_scr[(c - 1) * SLOTS : c * SLOTS] = wh
        wl_scr[(c - 1) * SLOTS : c * SLOTS] = wl
    wst = (wh_scr[...], wl_scr[...])
    dp += decay * pick_rows(dot3(wst, split2(gv), 1, 0), SLOTS, chunks, 1)
    carried = jnp.exp(levels + aux_ref[0, base + 1 : base + 2, :])
    dp += carried * dot3(vin, g, 1, 1)
    dz = SCALE * probs * (dp - jnp.sum(probs * dp, axis=0, keepdims=True))
    a_ref[...] = dz * sc_ref[...] + probs * dp

    def mixing(j, carry):
        d_scr[pl.ds(j, 1), :] = jnp.sum(w_scr[j] * dz, axis=0, keepdims=True)
        return carry

    lax.fori_loop(0, CHUNK, mixing, 0, unroll=8)
    row = lax.broadcasted_iota(jnp.int32, (tokens, tokens), 0) // CHUNK
    col = lax.broadcasted_iota(jnp.int32, (tokens, tokens), 1) // CHUNK
    mz_t = jnp.where(row == col, jnp.concatenate([d_scr[...]] * chunks, axis=0), 0.0)
    zst = split2(stack_chunks(dz * decay, chunks))
    pst = split2(stack_chunks(probs * decay, chunks))
    mz_t += dot3(wst, zst, 0, 0)
    mz = split2(mz_t)
    zc, pc = split2(dz * carried), split2(probs * carried)
    store_rows(gq_ref, (dot2(mz, k, 0, 0) + dot3(zc, kin, 0, 0)).astype(bf16))
    gk_ref[...] = dot2(mz, q, 1, 0)
    gv_ref[...] = dot3(split2(mt_ref[0]), g, 1, 0)
    grad_ks, grad_vs = dot2(zc, q, 1, 0), dot3(pc, g, 1, 0)
    store_state(d_ref, grad_ks, grad_vs)
    store_state(low_ref, grad_ks, grad_vs)
    qk = dg(q, k, 1, 1)
    gv_n = dot2(g, v, 1, 1)
    d_scr[...] = pick_rows(qk, CHUNK, chunks)
    e_scr[...] = pick_rows(gv_n, CHUNK, chunks)

    def onward(i, total):
        gap = group_lane(levels, i) - levels + aux_ref[0, pl.ds(CHUNK + i, 1), :]
        term = group_lane(dz, i) * d_scr[pl.ds(i, 1), :] + group_lane(probs, i) * e_scr[pl.ds(i, 1), :]
        return total + jnp.exp(gap) * term

    total = lax.fori_loop(0, CHUNK, onward, jnp.zeros_like(levels), unroll=8)
    cross = dot3(zst, split2(qk), 1, 0) + dot3(pst, split2(gv_n), 1, 0)
    for c in range(1, chunks):
        total += x_scr[(c - 1) * SLOTS : c * SLOTS] * cross[(c - 1) * SLOTS : c * SLOTS]
    r_ref[...] = total


def finish_kernel(
    k_ref, v_ref, lev_ref, one_ref, sig_ref, aux_ref, sums_ref, ki_ref, vi_ref, ks_ref, vs_ref, gk_ref, gv_ref,
    r_ref, a_ref, dk_ref, dv_ref, gko_ref, gvo_ref, gl_ref,
):
    tokens = lev_ref.shape[1]
    base, _ = aux_rows(tokens)
    levels, one = lev_ref[...], one_ref[...]
    k, v = rows_of(k_ref), rows_of(v_ref)
    tail = jnp.exp(levels[:, tokens - 1 : tokens] - levels + aux_ref[0, base + 2 : base + 3, :])
    end = jnp.exp(levels[:, tokens - 1 : tokens] + aux_ref[0, base + 1 : base + 2, tokens - 1 : tokens])
    dk, dv = dk_ref[0], dv_ref[0]
    dks, dvs = split2(dk), split2(dv)
    weights = split2(tail * one)
    store_rows(gko_ref, (gk_ref[...] + dot3(weights, dks, 0, 0)).astype(bf16))
    store_rows(gvo_ref, (gv_ref[...] + dot3(weights, dvs, 0, 0)).astype(bf16))
    rows = r_ref[...] + tail * (dot2(dks, k, 1, 1) + dot2(dvs, v, 1, 1))
    final_k = end * ki_ref[0] + ks_ref[0]
    final_v = end * vi_ref[0] + vs_ref[0]
    at_end = jnp.sum(dk * final_k + dv * final_v, axis=1, keepdims=True)
    x = a_ref[...] - one * rows
    high = x.astype(bf16)
    mid, low = split2(x - high.astype(f32))
    sums = sums_ref[0]
    flow = dg(high, sums, 1, 0) + (dg(mid, sums, 1, 0) + dg(low, sums, 1, 0))
    flow += jnp.where(aux_ref[0, base + 2 : base + 3, :] == 0.0, at_end, 0.0)
    grad = flow * aux_ref[0, base + 3 : base + 4, :] - (1.0 - one) * rows
    gl_ref[...] = (grad * sig_ref[...]).astype(bf16)


def seq_specs(tokens, members):
    def own(col):
        return pl.BlockSpec((members, 1, tokens // members, HEAD_DIM), lambda i: (0, i, 0, col))

    tok = pl.BlockSpec((tokens, HEAD_DIM), lambda i: (i, 0))
    lane = pl.BlockSpec((SLOTS, tokens), lambda i: (0, i))
    _, rows = aux_rows(tokens)
    aux = pl.BlockSpec((1, rows, tokens), lambda i: (i, 0, 0))
    state = pl.BlockSpec((1, SLOTS, 2 * HEAD_DIM), lambda i: (i, 0, 0))
    key_half = pl.BlockSpec((1, SLOTS, HEAD_DIM), lambda i: (i, 0, 0))
    value_half = pl.BlockSpec((1, SLOTS, HEAD_DIM), lambda i: (i, 0, 1))
    halves = [key_half, value_half]
    gain = pl.BlockSpec((1, HEAD_DIM), lambda i: (0, 0))
    square = pl.BlockSpec((1, tokens, tokens), lambda i: (i, 0, 0))
    row = pl.BlockSpec((1, 1, HEAD_DIM), lambda i: (i, 0, 0))
    return own, tok, lane, aux, state, halves, gain, square, row


def params(mib):
    return pltpu.CompilerParams(vmem_limit_bytes=mib << 20)


def cost(count, flops, size):
    return pl.CostEstimate(flops=count * flops, bytes_accessed=count * size, transcendentals=count * 1000000)


def shape(dims, dtype):
    return jax.ShapeDtypeStruct(dims, dtype)


def run_states(qkv, ld, one, aux):
    count, _, tokens = aux.shape
    own, tok, lane, auxs, state, _, _, _, _ = seq_specs(tokens, qkv.shape[0])
    return pl.pallas_call(
        state_kernel,
        grid=(count,),
        in_specs=[own(1), own(2), lane, lane, auxs],
        out_specs=[lane, state, state, pl.BlockSpec((1, SLOTS, 128), lambda i: (i, 0, 0))],
        out_shape=[
            shape((SLOTS, count * tokens), f32),
            shape((count, SLOTS, 2 * HEAD_DIM), f32),
            shape((count, SLOTS, 2 * HEAD_DIM), bf16),
            shape((count, SLOTS, 128), f32),
        ],
        compiler_params=params(24),
        cost_estimate=cost(count, 100000000, 1500000),
    )(qkv, qkv, ld, one, aux)


def big_scratch(tokens):
    stack = (tokens // CHUNK - 1) * SLOTS
    return stack


def run_forward(qkv, levels, one, aux, state_in, gain):
    count, _, tokens = aux.shape
    own, tok, lane, auxs, state, halves, gains, square, _ = seq_specs(tokens, qkv.shape[0])
    stack = big_scratch(tokens)
    return pl.pallas_call(
        forward_kernel,
        grid=(count,),
        in_specs=[own(0), own(1), own(2), lane, lane, auxs, *halves, gains],
        out_specs=[own(0), tok, lane, lane, square],
        out_shape=[
            shape(qkv.shape[:3] + (HEAD_DIM,), bf16),
            shape((count * tokens, HEAD_DIM), f32),
            shape((SLOTS, count * tokens), f32),
            shape((SLOTS, count * tokens), f32),
            shape((count, tokens, tokens), f32),
        ],
        scratch_shapes=[
            pltpu.VMEM((CHUNK, SLOTS, tokens), f32),
            pltpu.VMEM((CHUNK, tokens), f32),
            pltpu.VMEM((stack, tokens), bf16),
            pltpu.VMEM((stack, tokens), bf16),
        ],
        compiler_params=params(40),
        cost_estimate=cost(count, 1000000000, 3000000),
    )(qkv, qkv, qkv, levels, one, aux, state_in, state_in, gain)


def run_backward(qkv, levels, one, aux, state_in, gain, mixed, probs, scores, mixed_t, grad_o):
    count, _, tokens = aux.shape
    own, tok, lane, auxs, state, halves, gains, square, row = seq_specs(tokens, qkv.shape[0])
    stack = big_scratch(tokens)
    return pl.pallas_call(
        backward_kernel,
        grid=(count,),
        in_specs=[own(0), own(1), own(2), lane, lane, auxs, *halves, gains, tok, lane, lane, square, own(0)],
        out_specs=[own(0), tok, tok, lane, lane, state, state, row],
        out_shape=[
            shape(qkv.shape[:3] + (HEAD_DIM,), bf16),
            shape((count * tokens, HEAD_DIM), f32),
            shape((count * tokens, HEAD_DIM), f32),
            shape((SLOTS, count * tokens), f32),
            shape((SLOTS, count * tokens), f32),
            shape((count, SLOTS, 2 * HEAD_DIM), f32),
            shape((count, SLOTS, 2 * HEAD_DIM), bf16),
            shape((count, 1, HEAD_DIM), f32),
        ],
        scratch_shapes=[
            pltpu.VMEM((CHUNK, SLOTS, tokens), f32),
            pltpu.VMEM((CHUNK, tokens), f32),
            pltpu.VMEM((CHUNK, tokens), f32),
            pltpu.VMEM((stack, tokens), f32),
            pltpu.VMEM((stack, tokens), bf16),
            pltpu.VMEM((stack, tokens), bf16),
        ],
        compiler_params=params(48),
        cost_estimate=cost(count, 3000000000, 5000000),
    )(qkv, qkv, qkv, levels, one, aux, state_in, state_in, gain, mixed, probs, scores, mixed_t, grad_o)


def run_finish(qkv, levels, one, sig, aux, sums, state_in, state_own, gk, gv, rows, acts, grad_later):
    count, _, tokens = aux.shape
    own, tok, lane, auxs, state, halves, _, square, _ = seq_specs(tokens, qkv.shape[0])
    return pl.pallas_call(
        finish_kernel,
        grid=(count,),
        in_specs=[own(1), own(2), lane, lane, lane, auxs, square, *halves, *halves]
        + [tok, tok, lane, lane, *halves],
        out_specs=[own(0), own(0), lane],
        out_shape=[
            shape(qkv.shape[:3] + (HEAD_DIM,), bf16),
            shape(qkv.shape[:3] + (HEAD_DIM,), bf16),
            shape((SLOTS, count * tokens), bf16),
        ],
        compiler_params=params(40),
        cost_estimate=cost(count, 300000000, 4000000),
    )(
        qkv, qkv, levels, one, sig, aux, sums, state_in, state_in, state_own, state_own,
        gk, gv, rows, acts, grad_later, grad_later,
    )


def matmul(a, b, ca=1, cb=0):
    return lax.dot_general(a, b, (((ca,), (cb,)), ((), ())), preferred_element_type=f32)


def rms_parts(array, gain_vec):
    factor = lax.rsqrt(jnp.mean(array * array, axis=-1, keepdims=True) + epsilon)
    unit_val = array * factor
    return unit_val, factor, unit_val * gain_vec


def norm_back(unit_val, factor, grad_unit):
    return factor * (grad_unit - unit_val * jnp.mean(grad_unit * unit_val, axis=-1, keepdims=True))


def row_major(array):
    return with_layout_constraint(array, Layout(major_to_minor=tuple(range(array.ndim))))


def tie(*values):
    return lax.optimization_barrier(values)


def line_gather(parts, axis, buffer):
    size, here = lax.axis_size(axis), lax.axis_index(axis)
    count = parts.shape[0]
    moving = {to: [parts[c] for c in range(count)] for to in (1, -1)}
    for s in range(1, size):
        for c in range(count):
            for to in (1, -1):
                sources = range(s - 1, size - 1) if to == 1 else range(1, size - s + 1)
                value = lax.ppermute(moving[to][c], axis, [(i, i + to) for i in sources])
                moving[to][c] = value
                origin = here - s * to
                valid = (origin >= 0) & (origin < size)
                at = (jnp.where(valid, origin, here), c) + (0,) * (parts.ndim - 1)
                buffer = lax.dynamic_update_slice(buffer, value[None, None], at)
    return lax.dynamic_update_slice(buffer, parts[None], (here,) + (0,) * parts.ndim)


def per_device(
    layer_input, segments, cotangent, norm1_gain, norm2_gain, head_gain, decay_bias,
    w_query, w_key, w_value, w_decay, w_out, w_gate, w_up, w_down,
):
    count, tokens, width = layer_input.shape
    rows = count * tokens
    hidden_units = w_gate.shape[1]
    heads = w_query.shape[1]
    tp_place, here = lax.axis_index("tp"), lax.axis_index("ctx")
    swap_x = [(0, 1), (1, 0), (2, 3), (3, 2)]
    places, members = lax.axis_size("ctx"), lax.axis_size("tp")
    part = tokens // members

    def owner_first(array):
        array = array.reshape(count, members, part, width).transpose(1, 0, 2, 3)
        return array.reshape(rows, width)

    def natural(array):
        return array.reshape(members, count, part, width).transpose(1, 0, 2, 3)

    def lanes(array, order):
        array = array.reshape(array.shape[0], *order, part).transpose(0, 2, 1, 3)
        return array.reshape(array.shape[0], rows)

    def blocks_of(array):
        return array.reshape(members, count, part, -1)

    def mine(array):
        return lax.dynamic_slice_in_dim(array, tp_place * (count * part), count * part, 0)

    def to_shards(array):
        return lax.psum_scatter(array, "tp", scatter_dimension=0, tiled=True)

    def from_shards(array):
        return lax.all_gather(array.astype(bf16), "tp", axis=0, tiled=True)

    def gather_rows(array):
        return lax.all_gather(array, ("dp", "ctx"), axis=0, tiled=True)

    core, y, x_at = lax.axis_index("dp"), here // 2, here % 2
    swap_y = [(0, 2), (2, 0), (1, 3), (3, 1)]

    def pick(value, index, axis):
        return lax.dynamic_index_in_dim(value, index, axis, keepdims=False)

    def add(a, b, dtype=bf16):
        return row_major((a.astype(f32) + b.astype(f32)).astype(dtype))

    def scatter_cores(array):
        if places != 4:
            return (array,)
        array = row_major(array).reshape(2, 2, 2, array.shape[0] // 8, array.shape[1])
        other = lax.ppermute(pick(array, 1 - core, 0), "dp", [(0, 1), (1, 0)])
        return pick(array, core, 0), other

    def scatter_first(held):
        if places != 4:
            return held
        chip = add(*held)
        half = chip.shape[2] // 2
        upper, lower = chip[:, :, :half], chip[:, :, half:]
        return (
            pick(upper, x_at, 1),
            pick(lower, y, 0),
            lax.ppermute(pick(upper, 1 - x_at, 1), "ctx", swap_x),
            lax.ppermute(pick(lower, 1 - y, 0), "ctx", swap_y),
        )

    def scatter_second(held):
        if places != 4:
            return held
        upper, lower, over_x, over_y = held
        upper, lower = add(upper, over_x), add(lower, over_y)
        return (
            pick(upper, y, 0),
            pick(lower, x_at, 0),
            lax.ppermute(pick(upper, 1 - y, 0), "ctx", swap_y),
            lax.ppermute(pick(lower, 1 - x_at, 0), "ctx", swap_x),
        )

    def scatter_end(held):
        if places != 4:
            return lax.psum_scatter(
                held[0], ("dp", "ctx"), scatter_dimension=0, tiled=True
            ).astype(f32)
        upper, lower, over_y, over_x = held
        return row_major(jnp.concatenate([add(upper, over_y, f32), add(lower, over_x, f32)], axis=0))

    def gather_in_parts(array, parts):
        buffer = jnp.zeros((members, parts, count * part // parts, width), bf16)
        return line_gather(array.astype(bf16).reshape(buffer.shape[1:]), "tp", buffer).reshape(rows, width)

    def from_partner(array, distance):
        return lax.ppermute(array, "tp", [(i, i ^ distance) for i in range(members)])

    cut = 3 * heads
    w_in = gather_rows(jnp.concatenate([w_query, w_key, w_value, w_decay], axis=1))
    w_qkv, w_dec = w_in[:, :cut], w_in[:, cut:]
    w_out_t = w_out.T
    w_heads = gather_rows(
        jnp.concatenate([w_out_t] + [from_partner(w_out_t, r) for r in range(1, members)], axis=1)
    )
    w_rest = gather_rows(jnp.concatenate([w_gate, w_up, w_down.T], axis=1))
    w_gu = w_rest[:, : 2 * hidden_units]
    w_d = w_rest[:, 2 * hidden_units :]

    edges = lax.all_gather(jnp.stack([segments[:, 0], segments[:, -1]]), "ctx")
    prev_doc = jnp.where(here > 0, edges[jnp.maximum(here - 1, 0), 1], -1)
    aux = make_aux(segments, prev_doc)
    place = jnp.arange(tokens)
    sums = (
        (place[:, None] >= place[None, :])[None] & (segments[:, :, None] == segments[:, None, :])
    ).astype(bf16)
    index = jnp.arange(places)
    reach_in = (index[:, None] < here) & (edges[:, 1] == segments[:, 0])
    reach_out = (index[:, None] > here) & (edges[:, 0] == segments[:, -1])

    def flag(array):
        return array.astype(f32)[:, None, None]

    if places == 4:
        beside = here ^ 1
        is_low = x_at == 0

        def level_ends(own_end):
            return lax.ppermute(own_end, "ctx", swap_x)

        def exchange(own, low, forward, own_end, near_end):
            row = lax.dynamic_slice_in_dim(edges, 2 * y, 2, 0)
            if forward:
                reach, pairs, origin, side = reach_in, [(0, 2), (1, 3)], 1, 1
                through = jnp.where(is_low, near_end, own_end)
            else:
                reach, pairs, origin, side = reach_out, [(2, 0), (3, 1)], 2, 0
                through = jnp.where(is_low, own_end, near_end)
            near = lax.ppermute(low, "ctx", swap_x).astype(f32)
            keeps = flag(row[0, side] == row[1, side])
            keeps = (keeps * jnp.exp(through))[..., :1]
            outer = is_low if forward else ~is_low
            joined = jnp.where(outer, near + keeps * own, own + keeps * near)
            far = lax.ppermute(joined.astype(bf16), "ctx", pairs).astype(f32)
            distant = ~is_low if forward else is_low
            scale = jnp.where(distant, jnp.exp(near_end), 1.0)[..., :1]
            near_flag = flag(lax.dynamic_index_in_dim(reach, beside, 0, False))
            return near_flag * near + (flag(reach[origin]) * scale) * far

    else:
        between = (index[None, :] > jnp.minimum(index[:, None], here)) & (
            index[None, :] < jnp.maximum(index[:, None], here)
        )

        def level_ends(own_end):
            return own_end

        def exchange(own, low, forward, own_end, near_end):
            ends = lax.all_gather(own_end[..., :1], "ctx")
            span = jnp.where(between[:, :, None, None, None], ends[None], 0.0)
            span = jnp.exp(jnp.sum(span, axis=1))
            coefs = jnp.where((reach_in if forward else reach_out)[..., None, None], span, 0.0)
            return jnp.sum(lax.all_gather(own, "ctx") * coefs, axis=0)

    x = owner_first(layer_input)
    unit_one, factor_one, scaled_one = rms_parts(x.astype(f32), norm1_gain)
    normed1 = scaled_one.astype(bf16)
    qkv = blocks_of(matmul(normed1, w_qkv).astype(bf16))
    bias_here = lax.dynamic_slice_in_dim(decay_bias, tp_place * SLOTS, SLOTS)
    logits = lanes(matmul(w_dec, normed1, 0, 1), (members, count)) + bias_here[:, None]
    log_decay = jax.nn.log_sigmoid(logits) / gate_norm
    one = -jnp.expm1(log_decay)
    sig = jax.nn.sigmoid(-logits) / gate_norm
    levels, state_own, state_low, own_end = run_states(qkv, log_decay, one, aux)
    near_end = level_ends(own_end)
    state_in = exchange(state_own, state_low, True, own_end, near_end)
    gain = head_gain[None, :]
    normed_o, mixed, probs, scores, mixed_t = run_forward(qkv, levels, one, aux, state_in, gain)
    by_owner = normed_o.reshape(members, count * part, heads)

    def for_partner(r):
        return lax.dynamic_index_in_dim(by_owner, tp_place ^ r, 0, keepdims=False)

    normed_heads = jnp.concatenate(
        [for_partner(0)] + [from_partner(for_partner(r), r) for r in range(1, members)], axis=1
    )
    hidden = mine(x).astype(f32) + matmul(normed_heads, w_heads, 1, 1)
    unit_two, factor_two, scaled_two = rms_parts(hidden, norm2_gain)
    normed2 = gather_in_parts(scaled_two, 1)
    pre = matmul(normed2, w_gu)
    gate_pre, up_pre = pre[:, :hidden_units], pre[:, hidden_units:]
    gate_sig = jax.nn.sigmoid(gate_pre)
    gate_silu = gate_pre * gate_sig
    hidden_act = (gate_silu * up_pre).astype(bf16)

    grad_feed = owner_first(cotangent)
    grad_act = matmul(grad_feed, w_d)
    grad_gate = (grad_act * up_pre * gate_sig * (1.0 + gate_pre * (1.0 - gate_sig))).astype(bf16)
    grad_up = (grad_act * gate_silu).astype(bf16)
    grad_gu = jnp.concatenate([grad_gate, grad_up], axis=1)
    part_n2 = matmul(grad_gu, w_gu, 1, 1).astype(bf16)
    grad_n2 = to_shards(part_n2).astype(f32)
    held_wgu = scatter_cores(matmul(normed2, grad_gu, 0, 0).astype(bf16))
    held_wd = scatter_cores(matmul(grad_feed, hidden_act, 0, 0).astype(bf16))
    feed_part = matmul(hidden_act, w_d, 1, 1).astype(bf16)
    gain_two_part = jnp.sum(grad_n2 * unit_two, axis=0)
    grad_hidden = mine(grad_feed).astype(f32) + norm_back(unit_two, factor_two, grad_n2 * norm2_gain)
    grad_attn = grad_hidden.astype(bf16)
    sent = matmul(grad_attn, w_heads).astype(bf16)
    sent, held_wgu, held_wd = tie(sent, held_wgu, held_wd)
    feed = to_shards(feed_part)
    arrived = [sent[:, :heads]] + [
        from_partner(sent[:, r * heads : (r + 1) * heads], r) for r in range(1, members)
    ]
    held_wgu, held_wd = scatter_first(held_wgu), scatter_first(held_wd)
    grad_o = jnp.zeros((members, count * part, heads), bf16)
    for r in range(members):
        grad_o = lax.dynamic_update_slice(grad_o, arrived[r][None], (tp_place ^ r, 0, 0))
    grad_q, gk, gv, row_sums, acts, grad_state, grad_low, head_part = run_backward(
        qkv, levels, one, aux, state_in, gain, mixed, probs, scores, mixed_t, blocks_of(grad_o)
    )
    grad_low, feed, held_wgu, grad_attn = tie(grad_low, feed, held_wgu, grad_attn)
    out_shard = (hidden + feed.astype(f32)).astype(bf16)
    grad_low, out_shard = tie(grad_low, out_shard)
    output = from_shards(out_shard)
    grad_later = exchange(grad_state, grad_low, False, own_end, near_end)
    grad_k, grad_v, grad_logits = run_finish(
        qkv, levels, one, sig, aux, sums, state_in, state_own, gk, gv, row_sums, acts, grad_later
    )
    decay_rows = lanes(grad_logits, (count, members))
    grad_all = jnp.concatenate(
        [a.reshape(rows, heads) for a in (grad_q, grad_k, grad_v)] + [decay_rows.T], axis=1
    )
    part_n1 = (matmul(grad_all[:, :cut], w_qkv, 1, 1) + matmul(decay_rows, w_dec, 0, 1)).astype(bf16)
    part_n1, output, grad_all = tie(part_n1, output, grad_all)
    grad_n1 = to_shards(part_n1)
    gain_one_part = jnp.sum(part_n1.astype(f32) * unit_one, axis=0)
    bias_part = lax.dynamic_update_slice_in_dim(
        jnp.zeros_like(decay_bias),
        jnp.sum(grad_logits.astype(f32), axis=1),
        tp_place * SLOTS,
        0,
    )
    small = jnp.concatenate(
        [gain_one_part, gain_two_part, jnp.sum(head_part, axis=(0, 1)), bias_part]
    )
    held_wo = scatter_first(scatter_cores(matmul(grad_attn, normed_heads, 0, 0).astype(bf16)))
    grad_in = matmul(normed1, grad_all, 0, 0).astype(bf16)
    held_in = scatter_cores(grad_in)
    grad_n1, small, held_in, held_wd = tie(grad_n1, small, held_in, held_wd)
    held_wgu, held_wo = scatter_second(held_wgu), scatter_second(held_wo)
    input_grad = grad_hidden + norm_back(mine(unit_one), mine(factor_one), grad_n1.astype(f32) * norm1_gain)
    input_grad = from_shards(input_grad)
    held_wd = scatter_second(held_wd)
    if places != 4:
        small = lax.psum(small, ("dp", "ctx", "tp"))
    else:
        small += lax.ppermute(small, "dp", [(0, 1), (1, 0)])
        for axis in ("ctx", "tp"):
            for r in (1, 2):
                small += lax.ppermute(small, axis, [(i, i ^ r) for i in range(4)])
    held_in = scatter_first(held_in)
    rows_wo, rows_wgu, rows_wd = scatter_end(held_wo), scatter_end(held_wgu), scatter_end(held_wd)
    rows_att = scatter_end(scatter_second(held_in))
    rows_wo = rows_wo[:, :heads] + sum(
        from_partner(rows_wo[:, r * heads : (r + 1) * heads].astype(bf16), r).astype(f32)
        for r in range(1, members)
    )
    input_grad = natural(input_grad).astype(f32)
    return (
        natural(output).reshape(count, tokens, width),
        input_grad.reshape(count, tokens, width),
        small[:width],
        small[width : 2 * width],
        small[2 * width : 2 * width + HEAD_DIM],
        small[2 * width + HEAD_DIM :],
        rows_att[:, :heads],
        rows_att[:, heads : 2 * heads],
        rows_att[:, 2 * heads : cut],
        rows_att[:, cut:],
        rows_wo.T,
        rows_wgu[:, :hidden_units],
        rows_wgu[:, hidden_units:],
        rows_wd.T,
    )


def solution(mesh):
    return jax.shard_map(
        per_device,
        mesh=mesh,
        in_specs=(
            P("dp", "ctx", None),
            P("dp", "ctx"),
            P("dp", "ctx", None),
            P(),
            P(),
            P(),
            P(),
            P(("dp", "ctx"), "tp"),
            P(("dp", "ctx"), "tp"),
            P(("dp", "ctx"), "tp"),
            P(("dp", "ctx"), "tp"),
            P("tp", ("dp", "ctx")),
            P(("dp", "ctx"), "tp"),
            P(("dp", "ctx"), "tp"),
            P("tp", ("dp", "ctx")),
        ),
        out_specs=(
            P("dp", "ctx", None),
            P("dp", "ctx", None),
            P(),
            P(),
            P(),
            P(),
            P(("dp", "ctx"), "tp"),
            P(("dp", "ctx"), "tp"),
            P(("dp", "ctx"), "tp"),
            P(("dp", "ctx"), "tp"),
            P("tp", ("dp", "ctx")),
            P(("dp", "ctx"), "tp"),
            P(("dp", "ctx"), "tp"),
            P("tp", ("dp", "ctx")),
        ),
        check_vma=False,
    )
```

```python
import jax
import jax.numpy as jnp
from jax import lax
from jax.experimental import pallas as pl
from jax.experimental.layout import Layout, with_layout_constraint
from jax.experimental.pallas import tpu as pltpu
from jax.sharding import PartitionSpec as P

HEAD_DIM = 512
SLOTS = 64
CHUNK = 32
epsilon = 1e-05
gate_norm = 8.0
f32 = jnp.float32
bf16 = jnp.bfloat16
NEG = -1e30
SCALE = HEAD_DIM**-0.5


def split2(x):
    high = x.astype(bf16)
    return high, (x - high.astype(f32)).astype(bf16)


def dg(a, b, ca, cb):
    return lax.dot_general(a, b, (((ca,), (cb,)), ((), ())), preferred_element_type=f32)


def dot2(a, b, ca, cb):
    high, low = a
    return dg(high, b, ca, cb) + dg(low, b, ca, cb)


def dot2r(a, b, ca, cb):
    high, low = b
    return dg(a, high, ca, cb) + dg(a, low, ca, cb)


def dot3(a, b, ca, cb):
    return dg(a[0], b[0], ca, cb) + (dg(a[0], b[1], ca, cb) + dg(a[1], b[0], ca, cb))


def group_lane(x, index):
    rows, lanes = x.shape
    lane = lax.broadcasted_iota(jnp.int32, (rows, 128), 1)
    at = (lane // CHUNK) * CHUNK + index
    parts = [
        jnp.take_along_axis(x[:, i : i + 128], at, axis=1, mode="promise_in_bounds")
        for i in range(0, lanes, 128)
    ]
    return jnp.concatenate(parts, axis=1)


def chunk_of(rows, lanes):
    return lax.broadcasted_iota(jnp.int32, (rows, lanes), 1) // CHUNK


def pick_rows(array, rows, chunks, first=0):
    lanes = array.shape[1]
    chunk = chunk_of(rows, lanes)
    total = jnp.zeros((rows, lanes), f32)
    for c in range(first, chunks):
        total = jnp.where(chunk == c, array[(c - first) * rows : (c - first + 1) * rows], total)
    return total


def level_refs(levels):
    slots, tokens = levels.shape
    chunk = chunk_of(slots, tokens)
    refs = jnp.zeros_like(levels)
    for c in range(1, tokens // CHUNK):
        refs = jnp.where(chunk == c, levels[:, c * CHUNK - 1 : c * CHUNK], refs)
    return refs


def stack_chunks(array, chunks):
    chunk = chunk_of(*array.shape)
    return jnp.concatenate([jnp.where(chunk == c, array, 0.0) for c in range(1, chunks)], axis=0)


def rows_of(ref):
    return ref[...].reshape(-1, ref.shape[-1])


def store_rows(ref, value):
    ref[...] = value.reshape(ref.shape)


def store_state(ref, key_part, value_part):
    ref[0, :, :HEAD_DIM] = key_part.astype(ref.dtype)
    ref[0, :, HEAD_DIM:] = value_part.astype(ref.dtype)


def aux_rows(tokens):
    chunks = tokens // CHUNK
    base = 2 * CHUNK + chunks
    return base, base + 8


def make_aux(seg, prev_doc):
    count, tokens = seg.shape
    chunks = tokens // CHUNK
    place = jnp.arange(tokens)
    local = place % CHUNK
    grouped = seg.reshape(count, chunks, CHUNK)
    spread = jnp.repeat(grouped.transpose(0, 2, 1), CHUNK, axis=2)
    index = jnp.arange(CHUNK)[:, None]
    same = spread == seg[:, None, :]
    from_j = same & (local[None, :] >= index)[None]
    to_i = same & (local[None, :] <= index)[None]
    ends = jnp.concatenate([jnp.full((count, 1), -5, seg.dtype), grouped[:, :-1, -1]], axis=1)
    before = (ends[:, :, None] == seg[:, None, :]) & (
        place[None, :] < (jnp.arange(chunks) * CHUNK)[:, None]
    )[None]
    after = jnp.repeat(ends, CHUNK, axis=1) == seg
    first = seg == seg[:, :1]
    last = seg == seg[:, -1:]
    bias = jnp.concatenate(
        [from_j, to_i, before, after[:, None], first[:, None], last[:, None]], axis=1
    )
    bias = jnp.where(bias, 0.0, NEG).astype(f32)
    previous = jnp.concatenate([prev_doc[:, None], seg[:, :-1]], axis=1)
    keeps = (previous == seg).astype(f32)[:, None]
    pad = jnp.zeros((count, 4, tokens), f32)
    return jnp.concatenate([bias, keeps, pad], axis=1)


def state_kernel(k_ref, v_ref, ld_ref, one_ref, aux_ref, lev_ref, st_ref, low_ref, end_ref):
    tokens = ld_ref.shape[1]
    base, _ = aux_rows(tokens)
    earlier = lax.broadcasted_iota(jnp.int32, (tokens, tokens), 0)
    later = lax.broadcasted_iota(jnp.int32, (tokens, tokens), 1)
    upper = jnp.where(earlier <= later, 1.0, 0.0).astype(bf16)
    ld = ld_ref[...]
    high, rest = ld.astype(bf16), None
    rest = ld - high.astype(f32)
    mid, low = split2(rest)
    levels = dg(high, upper, 1, 0) + (dg(mid, upper, 1, 0) + dg(low, upper, 1, 0))
    lev_ref[...] = levels
    tail = jnp.exp(levels[:, tokens - 1 : tokens] - levels + aux_ref[0, base + 2 : base + 3, :])
    tail = split2(tail * one_ref[...])
    state_k, state_v = dot2(tail, rows_of(k_ref), 1, 0), dot2(tail, rows_of(v_ref), 1, 0)
    store_state(st_ref, state_k, state_v)
    store_state(low_ref, state_k, state_v)
    end_ref[0] = jnp.broadcast_to(levels[:, tokens - 1 : tokens], (SLOTS, 128))


def forward_kernel(
    q_ref, k_ref, v_ref, lev_ref, one_ref, aux_ref, ki_ref, vi_ref, gain_ref,
    no_ref, mix_ref, p_ref, sc_ref, mt_ref, w_scr, d_scr, wh_scr, wl_scr,
):
    tokens = lev_ref.shape[1]
    chunks = tokens // CHUNK
    base, _ = aux_rows(tokens)
    levels, one = lev_ref[...], one_ref[...]
    q, k, v = rows_of(q_ref), rows_of(k_ref), rows_of(v_ref)
    chunk = chunk_of(SLOTS, tokens)
    kq = dg(k, q, 1, 1)
    d_scr[...] = pick_rows(kq, CHUNK, chunks)

    def inside(j, scores):
        gap = levels - group_lane(levels, j) + aux_ref[0, pl.ds(j, 1), :]
        w = jnp.exp(gap) * group_lane(one, j)
        w_scr[j] = w
        return scores + w * d_scr[pl.ds(j, 1), :]

    scores = lax.fori_loop(0, CHUNK, inside, jnp.zeros_like(levels), unroll=16)
    decay = jnp.exp(levels - level_refs(levels) + aux_ref[0, base : base + 1, :])
    for c in range(1, chunks):
        w = levels[:, c * CHUNK - 1 : c * CHUNK] - levels + aux_ref[0, 2 * CHUNK + c : 2 * CHUNK + c + 1, :]
        wh, wl = split2(jnp.exp(w) * one)
        wh_scr[(c - 1) * SLOTS : c * SLOTS] = wh
        wl_scr[(c - 1) * SLOTS : c * SLOTS] = wl
    wst = (wh_scr[...], wl_scr[...])
    scores += decay * pick_rows(dot3(wst, split2(kq), 1, 0), SLOTS, chunks, 1)
    carried = jnp.exp(levels + aux_ref[0, base + 1 : base + 2, :])
    scores += carried * dot2(split2(ki_ref[0]), q, 1, 1)
    sc_ref[...] = scores
    z = scores * SCALE
    e = jnp.exp(z - jnp.max(z, axis=0, keepdims=True))
    probs = e / jnp.sum(e, axis=0, keepdims=True)
    p_ref[...] = probs

    def mixing(j, carry):
        d_scr[pl.ds(j, 1), :] = jnp.sum(w_scr[j] * probs, axis=0, keepdims=True)
        return carry

    lax.fori_loop(0, CHUNK, mixing, 0, unroll=16)
    row = lax.broadcasted_iota(jnp.int32, (tokens, tokens), 0) // CHUNK
    col = lax.broadcasted_iota(jnp.int32, (tokens, tokens), 1) // CHUNK
    mixed_t = jnp.where(row == col, jnp.concatenate([d_scr[...]] * chunks, axis=0), 0.0)
    mixed_t += dot3(wst, split2(stack_chunks(probs * decay, chunks)), 0, 0)
    mt_ref[0] = mixed_t
    out = dot2(split2(mixed_t), v, 0, 0) + dot3(split2(probs * carried), split2(vi_ref[0]), 0, 0)
    mix_ref[...] = out
    unit = out * lax.rsqrt(jnp.mean(out * out, axis=1, keepdims=True) + epsilon)
    store_rows(no_ref, (unit * gain_ref[...]).astype(bf16))


def backward_kernel(
    q_ref, k_ref, v_ref, lev_ref, one_ref, aux_ref, ki_ref, vi_ref, gain_ref, mix_ref, p_ref, sc_ref, mt_ref, go_ref,
    gq_ref, gk_ref, gv_ref, r_ref, a_ref, d_ref, low_ref, hg_ref, w_scr, d_scr, e_scr, x_scr, wh_scr, wl_scr,
):
    tokens = lev_ref.shape[1]
    chunks = tokens // CHUNK
    base, _ = aux_rows(tokens)
    levels, one, probs = lev_ref[...], one_ref[...], p_ref[...]
    q, k, v = rows_of(q_ref), rows_of(k_ref), rows_of(v_ref)
    out, go = mix_ref[...], rows_of(go_ref).astype(f32)
    factor = lax.rsqrt(jnp.mean(out * out, axis=1, keepdims=True) + epsilon)
    unit = out * factor
    hg_ref[0] = jnp.sum(go * unit, axis=0, keepdims=True)
    go = go * gain_ref[...]
    grad = factor * (go - unit * jnp.mean(go * unit, axis=1, keepdims=True))
    g = split2(grad)
    kin, vin = split2(ki_ref[0]), split2(vi_ref[0])
    gv = dot2r(v, g, 1, 1)
    d_scr[...] = pick_rows(gv, CHUNK, chunks)

    def inside(j, dp):
        gap = levels - group_lane(levels, j) + aux_ref[0, pl.ds(j, 1), :]
        w = jnp.exp(gap) * group_lane(one, j)
        w_scr[j] = w
        return dp + w * d_scr[pl.ds(j, 1), :]

    dp = lax.fori_loop(0, CHUNK, inside, jnp.zeros_like(levels), unroll=16)
    decay = jnp.exp(levels - level_refs(levels) + aux_ref[0, base : base + 1, :])
    for c in range(1, chunks):
        w = levels[:, c * CHUNK - 1 : c * CHUNK] - levels + aux_ref[0, 2 * CHUNK + c : 2 * CHUNK + c + 1, :]
        w = jnp.exp(w)
        x_scr[(c - 1) * SLOTS : c * SLOTS] = w
        wh, wl = split2(w * one)
        wh_scr[(c - 1) * SLOTS : c * SLOTS] = wh
        wl_scr[(c - 1) * SLOTS : c * SLOTS] = wl
    wst = (wh_scr[...], wl_scr[...])
    dp += decay * pick_rows(dot3(wst, split2(gv), 1, 0), SLOTS, chunks, 1)
    carried = jnp.exp(levels + aux_ref[0, base + 1 : base + 2, :])
    dp += carried * dot3(vin, g, 1, 1)
    dz = SCALE * probs * (dp - jnp.sum(probs * dp, axis=0, keepdims=True))
    a_ref[...] = dz * sc_ref[...] + probs * dp

    def mixing(j, carry):
        d_scr[pl.ds(j, 1), :] = jnp.sum(w_scr[j] * dz, axis=0, keepdims=True)
        return carry

    lax.fori_loop(0, CHUNK, mixing, 0, unroll=16)
    row = lax.broadcasted_iota(jnp.int32, (tokens, tokens), 0) // CHUNK
    col = lax.broadcasted_iota(jnp.int32, (tokens, tokens), 1) // CHUNK
    mz_t = jnp.where(row == col, jnp.concatenate([d_scr[...]] * chunks, axis=0), 0.0)
    zst = split2(stack_chunks(dz * decay, chunks))
    pst = split2(stack_chunks(probs * decay, chunks))
    mz_t += dot3(wst, zst, 0, 0)
    mz = split2(mz_t)
    zc, pc = split2(dz * carried), split2(probs * carried)
    store_rows(gq_ref, (dot2(mz, k, 0, 0) + dot3(zc, kin, 0, 0)).astype(bf16))
    gk_ref[...] = dot2(mz, q, 1, 0)
    gv_ref[...] = dot3(split2(mt_ref[0]), g, 1, 0)
    grad_ks, grad_vs = dot2(zc, q, 1, 0), dot3(pc, g, 1, 0)
    store_state(d_ref, grad_ks, grad_vs)
    store_state(low_ref, grad_ks, grad_vs)
    qk = dg(q, k, 1, 1)
    gv_n = dot2(g, v, 1, 1)
    d_scr[...] = pick_rows(qk, CHUNK, chunks)
    e_scr[...] = pick_rows(gv_n, CHUNK, chunks)

    def onward(i, total):
        gap = group_lane(levels, i) - levels + aux_ref[0, pl.ds(CHUNK + i, 1), :]
        term = group_lane(dz, i) * d_scr[pl.ds(i, 1), :] + group_lane(probs, i) * e_scr[pl.ds(i, 1), :]
        return total + jnp.exp(gap) * term

    total = lax.fori_loop(0, CHUNK, onward, jnp.zeros_like(levels), unroll=16)
    cross = dot3(zst, split2(qk), 1, 0) + dot3(pst, split2(gv_n), 1, 0)
    for c in range(1, chunks):
        total += x_scr[(c - 1) * SLOTS : c * SLOTS] * cross[(c - 1) * SLOTS : c * SLOTS]
    r_ref[...] = total


def finish_kernel(
    k_ref, v_ref, lev_ref, one_ref, sig_ref, aux_ref, sums_ref, ki_ref, vi_ref, ks_ref, vs_ref, gk_ref, gv_ref,
    r_ref, a_ref, dk_ref, dv_ref, gko_ref, gvo_ref, gl_ref,
):
    tokens = lev_ref.shape[1]
    base, _ = aux_rows(tokens)
    levels, one = lev_ref[...], one_ref[...]
    k, v = rows_of(k_ref), rows_of(v_ref)
    tail = jnp.exp(levels[:, tokens - 1 : tokens] - levels + aux_ref[0, base + 2 : base + 3, :])
    end = jnp.exp(levels[:, tokens - 1 : tokens] + aux_ref[0, base + 1 : base + 2, tokens - 1 : tokens])
    dk, dv = dk_ref[0], dv_ref[0]
    dks, dvs = split2(dk), split2(dv)
    weights = split2(tail * one)
    store_rows(gko_ref, (gk_ref[...] + dot3(weights, dks, 0, 0)).astype(bf16))
    store_rows(gvo_ref, (gv_ref[...] + dot3(weights, dvs, 0, 0)).astype(bf16))
    rows = r_ref[...] + tail * (dot2(dks, k, 1, 1) + dot2(dvs, v, 1, 1))
    final_k = end * ki_ref[0] + ks_ref[0]
    final_v = end * vi_ref[0] + vs_ref[0]
    at_end = jnp.sum(dk * final_k + dv * final_v, axis=1, keepdims=True)
    x = a_ref[...] - one * rows
    high = x.astype(bf16)
    mid, low = split2(x - high.astype(f32))
    sums = sums_ref[0]
    flow = dg(high, sums, 1, 0) + (dg(mid, sums, 1, 0) + dg(low, sums, 1, 0))
    flow += jnp.where(aux_ref[0, base + 2 : base + 3, :] == 0.0, at_end, 0.0)
    grad = flow * aux_ref[0, base + 3 : base + 4, :] - (1.0 - one) * rows
    gl_ref[...] = (grad * sig_ref[...]).astype(bf16)


def seq_specs(tokens, members):
    def own(col):
        return pl.BlockSpec((members, 1, tokens // members, HEAD_DIM), lambda i: (0, i, 0, col))

    tok = pl.BlockSpec((tokens, HEAD_DIM), lambda i: (i, 0))
    lane = pl.BlockSpec((SLOTS, tokens), lambda i: (0, i))
    _, rows = aux_rows(tokens)
    aux = pl.BlockSpec((1, rows, tokens), lambda i: (i, 0, 0))
    state = pl.BlockSpec((1, SLOTS, 2 * HEAD_DIM), lambda i: (i, 0, 0))
    key_half = pl.BlockSpec((1, SLOTS, HEAD_DIM), lambda i: (i, 0, 0))
    value_half = pl.BlockSpec((1, SLOTS, HEAD_DIM), lambda i: (i, 0, 1))
    halves = [key_half, value_half]
    gain = pl.BlockSpec((1, HEAD_DIM), lambda i: (0, 0))
    square = pl.BlockSpec((1, tokens, tokens), lambda i: (i, 0, 0))
    row = pl.BlockSpec((1, 1, HEAD_DIM), lambda i: (i, 0, 0))
    return own, tok, lane, aux, state, halves, gain, square, row


def params(mib):
    return pltpu.CompilerParams(vmem_limit_bytes=mib << 20)


def cost(count, flops, size):
    return pl.CostEstimate(flops=count * flops, bytes_accessed=count * size, transcendentals=count * 1000000)


def shape(dims, dtype):
    return jax.ShapeDtypeStruct(dims, dtype)


def run_states(qkv, ld, one, aux):
    count, _, tokens = aux.shape
    own, tok, lane, auxs, state, _, _, _, _ = seq_specs(tokens, qkv.shape[0])
    return pl.pallas_call(
        state_kernel,
        grid=(count,),
        in_specs=[own(1), own(2), lane, lane, auxs],
        out_specs=[lane, state, state, pl.BlockSpec((1, SLOTS, 128), lambda i: (i, 0, 0))],
        out_shape=[
            shape((SLOTS, count * tokens), f32),
            shape((count, SLOTS, 2 * HEAD_DIM), f32),
            shape((count, SLOTS, 2 * HEAD_DIM), bf16),
            shape((count, SLOTS, 128), f32),
        ],
        compiler_params=params(24),
        cost_estimate=cost(count, 100000000, 1500000),
    )(qkv, qkv, ld, one, aux)


def big_scratch(tokens):
    stack = (tokens // CHUNK - 1) * SLOTS
    return stack


def run_forward(qkv, levels, one, aux, state_in, gain):
    count, _, tokens = aux.shape
    own, tok, lane, auxs, state, halves, gains, square, _ = seq_specs(tokens, qkv.shape[0])
    stack = big_scratch(tokens)
    return pl.pallas_call(
        forward_kernel,
        grid=(count,),
        in_specs=[own(0), own(1), own(2), lane, lane, auxs, *halves, gains],
        out_specs=[own(0), tok, lane, lane, square],
        out_shape=[
            shape(qkv.shape[:3] + (HEAD_DIM,), bf16),
            shape((count * tokens, HEAD_DIM), f32),
            shape((SLOTS, count * tokens), f32),
            shape((SLOTS, count * tokens), f32),
            shape((count, tokens, tokens), f32),
        ],
        scratch_shapes=[
            pltpu.VMEM((CHUNK, SLOTS, tokens), f32),
            pltpu.VMEM((CHUNK, tokens), f32),
            pltpu.VMEM((stack, tokens), bf16),
            pltpu.VMEM((stack, tokens), bf16),
        ],
        compiler_params=params(40),
        cost_estimate=cost(count, 1000000000, 3000000),
    )(qkv, qkv, qkv, levels, one, aux, state_in, state_in, gain)


def run_backward(qkv, levels, one, aux, state_in, gain, mixed, probs, scores, mixed_t, grad_o):
    count, _, tokens = aux.shape
    own, tok, lane, auxs, state, halves, gains, square, row = seq_specs(tokens, qkv.shape[0])
    stack = big_scratch(tokens)
    return pl.pallas_call(
        backward_kernel,
        grid=(count,),
        in_specs=[own(0), own(1), own(2), lane, lane, auxs, *halves, gains, tok, lane, lane, square, own(0)],
        out_specs=[own(0), tok, tok, lane, lane, state, state, row],
        out_shape=[
            shape(qkv.shape[:3] + (HEAD_DIM,), bf16),
            shape((count * tokens, HEAD_DIM), f32),
            shape((count * tokens, HEAD_DIM), f32),
            shape((SLOTS, count * tokens), f32),
            shape((SLOTS, count * tokens), f32),
            shape((count, SLOTS, 2 * HEAD_DIM), f32),
            shape((count, SLOTS, 2 * HEAD_DIM), bf16),
            shape((count, 1, HEAD_DIM), f32),
        ],
        scratch_shapes=[
            pltpu.VMEM((CHUNK, SLOTS, tokens), f32),
            pltpu.VMEM((CHUNK, tokens), f32),
            pltpu.VMEM((CHUNK, tokens), f32),
            pltpu.VMEM((stack, tokens), f32),
            pltpu.VMEM((stack, tokens), bf16),
            pltpu.VMEM((stack, tokens), bf16),
        ],
        compiler_params=params(48),
        cost_estimate=cost(count, 3000000000, 5000000),
    )(qkv, qkv, qkv, levels, one, aux, state_in, state_in, gain, mixed, probs, scores, mixed_t, grad_o)


def run_finish(qkv, levels, one, sig, aux, sums, state_in, state_own, gk, gv, rows, acts, grad_later):
    count, _, tokens = aux.shape
    own, tok, lane, auxs, state, halves, _, square, _ = seq_specs(tokens, qkv.shape[0])
    return pl.pallas_call(
        finish_kernel,
        grid=(count,),
        in_specs=[own(1), own(2), lane, lane, lane, auxs, square, *halves, *halves]
        + [tok, tok, lane, lane, *halves],
        out_specs=[own(0), own(0), lane],
        out_shape=[
            shape(qkv.shape[:3] + (HEAD_DIM,), bf16),
            shape(qkv.shape[:3] + (HEAD_DIM,), bf16),
            shape((SLOTS, count * tokens), bf16),
        ],
        compiler_params=params(40),
        cost_estimate=cost(count, 300000000, 4000000),
    )(
        qkv, qkv, levels, one, sig, aux, sums, state_in, state_in, state_own, state_own,
        gk, gv, rows, acts, grad_later, grad_later,
    )


def matmul(a, b, ca=1, cb=0):
    return lax.dot_general(a, b, (((ca,), (cb,)), ((), ())), preferred_element_type=f32)


def rms_parts(array, gain_vec):
    factor = lax.rsqrt(jnp.mean(array * array, axis=-1, keepdims=True) + epsilon)
    unit_val = array * factor
    return unit_val, factor, unit_val * gain_vec


def norm_back(unit_val, factor, grad_unit):
    return factor * (grad_unit - unit_val * jnp.mean(grad_unit * unit_val, axis=-1, keepdims=True))


def row_major(array):
    return with_layout_constraint(array, Layout(major_to_minor=tuple(range(array.ndim))))


def tie(*values):
    return lax.optimization_barrier(values)


def line_gather(parts, axis, buffer):
    size, here = lax.axis_size(axis), lax.axis_index(axis)
    count = parts.shape[0]
    moving = {to: [parts[c] for c in range(count)] for to in (1, -1)}
    for s in range(1, size):
        for c in range(count):
            for to in (1, -1):
                sources = range(s - 1, size - 1) if to == 1 else range(1, size - s + 1)
                value = lax.ppermute(moving[to][c], axis, [(i, i + to) for i in sources])
                moving[to][c] = value
                origin = here - s * to
                valid = (origin >= 0) & (origin < size)
                at = (jnp.where(valid, origin, here), c) + (0,) * (parts.ndim - 1)
                buffer = lax.dynamic_update_slice(buffer, value[None, None], at)
    return lax.dynamic_update_slice(buffer, parts[None], (here,) + (0,) * parts.ndim)


def per_device(
    layer_input, segments, cotangent, norm1_gain, norm2_gain, head_gain, decay_bias,
    w_query, w_key, w_value, w_decay, w_out, w_gate, w_up, w_down,
):
    count, tokens, width = layer_input.shape
    rows = count * tokens
    hidden_units = w_gate.shape[1]
    heads = w_query.shape[1]
    tp_place, here = lax.axis_index("tp"), lax.axis_index("ctx")
    swap_x = [(0, 1), (1, 0), (2, 3), (3, 2)]
    places, members = lax.axis_size("ctx"), lax.axis_size("tp")
    part = tokens // members

    def owner_first(array):
        array = array.reshape(count, members, part, width).transpose(1, 0, 2, 3)
        return array.reshape(rows, width)

    def natural(array):
        return array.reshape(members, count, part, width).transpose(1, 0, 2, 3)

    def lanes(array, order):
        array = array.reshape(array.shape[0], *order, part).transpose(0, 2, 1, 3)
        return array.reshape(array.shape[0], rows)

    def blocks_of(array):
        return array.reshape(members, count, part, -1)

    def mine(array):
        return lax.dynamic_slice_in_dim(array, tp_place * (count * part), count * part, 0)

    def to_shards(array):
        return lax.psum_scatter(array, "tp", scatter_dimension=0, tiled=True)

    def from_shards(array):
        return lax.all_gather(array.astype(bf16), "tp", axis=0, tiled=True)

    def gather_rows(array):
        return lax.all_gather(array, ("dp", "ctx"), axis=0, tiled=True)

    core, y, x_at = lax.axis_index("dp"), here // 2, here % 2
    swap_y = [(0, 2), (2, 0), (1, 3), (3, 1)]

    def pick(value, index, axis):
        return lax.dynamic_index_in_dim(value, index, axis, keepdims=False)

    def add(a, b, dtype=bf16):
        return row_major((a.astype(f32) + b.astype(f32)).astype(dtype))

    def scatter_cores(array):
        if places != 4:
            return (array,)
        array = row_major(array).reshape(2, 2, 2, array.shape[0] // 8, array.shape[1])
        other = lax.ppermute(pick(array, 1 - core, 0), "dp", [(0, 1), (1, 0)])
        return pick(array, core, 0), other

    def scatter_first(held):
        if places != 4:
            return held
        chip = add(*held)
        half = chip.shape[2] // 2
        upper, lower = chip[:, :, :half], chip[:, :, half:]
        return (
            pick(upper, x_at, 1),
            pick(lower, y, 0),
            lax.ppermute(pick(upper, 1 - x_at, 1), "ctx", swap_x),
            lax.ppermute(pick(lower, 1 - y, 0), "ctx", swap_y),
        )

    def scatter_second(held):
        if places != 4:
            return held
        upper, lower, over_x, over_y = held
        upper, lower = add(upper, over_x), add(lower, over_y)
        return (
            pick(upper, y, 0),
            pick(lower, x_at, 0),
            lax.ppermute(pick(upper, 1 - y, 0), "ctx", swap_y),
            lax.ppermute(pick(lower, 1 - x_at, 0), "ctx", swap_x),
        )

    def scatter_end(held):
        if places != 4:
            return lax.psum_scatter(
                held[0], ("dp", "ctx"), scatter_dimension=0, tiled=True
            ).astype(f32)
        upper, lower, over_y, over_x = held
        return row_major(jnp.concatenate([add(upper, over_y, f32), add(lower, over_x, f32)], axis=0))

    def gather_in_parts(array, parts):
        buffer = jnp.zeros((members, parts, count * part // parts, width), bf16)
        return line_gather(array.astype(bf16).reshape(buffer.shape[1:]), "tp", buffer).reshape(rows, width)

    def from_partner(array, distance):
        return lax.ppermute(array, "tp", [(i, i ^ distance) for i in range(members)])

    cut = 3 * heads
    w_in = gather_rows(jnp.concatenate([w_query, w_key, w_value, w_decay], axis=1))
    w_qkv, w_dec = w_in[:, :cut], w_in[:, cut:]
    w_out_t = w_out.T
    w_heads = gather_rows(
        jnp.concatenate([w_out_t] + [from_partner(w_out_t, r) for r in range(1, members)], axis=1)
    )
    w_rest = gather_rows(jnp.concatenate([w_gate, w_up, w_down.T], axis=1))
    w_gu = w_rest[:, : 2 * hidden_units]
    w_d = w_rest[:, 2 * hidden_units :]

    edges = lax.all_gather(jnp.stack([segments[:, 0], segments[:, -1]]), "ctx")
    prev_doc = jnp.where(here > 0, edges[jnp.maximum(here - 1, 0), 1], -1)
    aux = make_aux(segments, prev_doc)
    place = jnp.arange(tokens)
    sums = (
        (place[:, None] >= place[None, :])[None] & (segments[:, :, None] == segments[:, None, :])
    ).astype(bf16)
    index = jnp.arange(places)
    reach_in = (index[:, None] < here) & (edges[:, 1] == segments[:, 0])
    reach_out = (index[:, None] > here) & (edges[:, 0] == segments[:, -1])

    def flag(array):
        return array.astype(f32)[:, None, None]

    if places == 4:
        beside = here ^ 1
        is_low = x_at == 0

        def level_ends(own_end):
            return lax.ppermute(own_end, "ctx", swap_x)

        def exchange(own, low, forward, own_end, near_end):
            row = lax.dynamic_slice_in_dim(edges, 2 * y, 2, 0)
            if forward:
                reach, pairs, origin, side = reach_in, [(0, 2), (1, 3)], 1, 1
                through = jnp.where(is_low, near_end, own_end)
            else:
                reach, pairs, origin, side = reach_out, [(2, 0), (3, 1)], 2, 0
                through = jnp.where(is_low, own_end, near_end)
            near = lax.ppermute(low, "ctx", swap_x).astype(f32)
            keeps = flag(row[0, side] == row[1, side])
            keeps = (keeps * jnp.exp(through))[..., :1]
            outer = is_low if forward else ~is_low
            joined = jnp.where(outer, near + keeps * own, own + keeps * near)
            far = lax.ppermute(joined.astype(bf16), "ctx", pairs).astype(f32)
            distant = ~is_low if forward else is_low
            scale = jnp.where(distant, jnp.exp(near_end), 1.0)[..., :1]
            near_flag = flag(lax.dynamic_index_in_dim(reach, beside, 0, False))
            return near_flag * near + (flag(reach[origin]) * scale) * far

    else:
        between = (index[None, :] > jnp.minimum(index[:, None], here)) & (
            index[None, :] < jnp.maximum(index[:, None], here)
        )

        def level_ends(own_end):
            return own_end

        def exchange(own, low, forward, own_end, near_end):
            ends = lax.all_gather(own_end[..., :1], "ctx")
            span = jnp.where(between[:, :, None, None, None], ends[None], 0.0)
            span = jnp.exp(jnp.sum(span, axis=1))
            coefs = jnp.where((reach_in if forward else reach_out)[..., None, None], span, 0.0)
            return jnp.sum(lax.all_gather(own, "ctx") * coefs, axis=0)

    x = owner_first(layer_input)
    unit_one, factor_one, scaled_one = rms_parts(x.astype(f32), norm1_gain)
    normed1 = scaled_one.astype(bf16)
    qkv = blocks_of(matmul(normed1, w_qkv).astype(bf16))
    bias_here = lax.dynamic_slice_in_dim(decay_bias, tp_place * SLOTS, SLOTS)
    logits = lanes(matmul(w_dec, normed1, 0, 1), (members, count)) + bias_here[:, None]
    log_decay = jax.nn.log_sigmoid(logits) / gate_norm
    one = -jnp.expm1(log_decay)
    sig = jax.nn.sigmoid(-logits) / gate_norm
    levels, state_own, state_low, own_end = run_states(qkv, log_decay, one, aux)
    near_end = level_ends(own_end)
    state_in = exchange(state_own, state_low, True, own_end, near_end)
    gain = head_gain[None, :]
    normed_o, mixed, probs, scores, mixed_t = run_forward(qkv, levels, one, aux, state_in, gain)
    by_owner = normed_o.reshape(members, count * part, heads)

    def for_partner(r):
        return lax.dynamic_index_in_dim(by_owner, tp_place ^ r, 0, keepdims=False)

    normed_heads = jnp.concatenate(
        [for_partner(0)] + [from_partner(for_partner(r), r) for r in range(1, members)], axis=1
    )
    hidden = mine(x).astype(f32) + matmul(normed_heads, w_heads, 1, 1)
    unit_two, factor_two, scaled_two = rms_parts(hidden, norm2_gain)
    normed2 = gather_in_parts(scaled_two, 1)
    pre = matmul(normed2, w_gu)
    gate_pre, up_pre = pre[:, :hidden_units], pre[:, hidden_units:]
    gate_sig = jax.nn.sigmoid(gate_pre)
    gate_silu = gate_pre * gate_sig
    hidden_act = (gate_silu * up_pre).astype(bf16)

    grad_feed = owner_first(cotangent)
    grad_act = matmul(grad_feed, w_d)
    grad_gate = (grad_act * up_pre * gate_sig * (1.0 + gate_pre * (1.0 - gate_sig))).astype(bf16)
    grad_up = (grad_act * gate_silu).astype(bf16)
    grad_gu = jnp.concatenate([grad_gate, grad_up], axis=1)
    part_n2 = matmul(grad_gu, w_gu, 1, 1).astype(bf16)
    grad_n2 = to_shards(part_n2).astype(f32)
    held_wgu = scatter_cores(matmul(normed2, grad_gu, 0, 0).astype(bf16))
    held_wd = scatter_cores(matmul(grad_feed, hidden_act, 0, 0).astype(bf16))
    feed_part = matmul(hidden_act, w_d, 1, 1).astype(bf16)
    gain_two_part = jnp.sum(grad_n2 * unit_two, axis=0)
    grad_hidden = mine(grad_feed).astype(f32) + norm_back(unit_two, factor_two, grad_n2 * norm2_gain)
    grad_attn = grad_hidden.astype(bf16)
    sent = matmul(grad_attn, w_heads).astype(bf16)
    sent, held_wgu, held_wd = tie(sent, held_wgu, held_wd)
    feed = to_shards(feed_part)
    arrived = [sent[:, :heads]] + [
        from_partner(sent[:, r * heads : (r + 1) * heads], r) for r in range(1, members)
    ]
    held_wgu, held_wd = scatter_first(held_wgu), scatter_first(held_wd)
    grad_o = jnp.zeros((members, count * part, heads), bf16)
    for r in range(members):
        grad_o = lax.dynamic_update_slice(grad_o, arrived[r][None], (tp_place ^ r, 0, 0))
    grad_q, gk, gv, row_sums, acts, grad_state, grad_low, head_part = run_backward(
        qkv, levels, one, aux, state_in, gain, mixed, probs, scores, mixed_t, blocks_of(grad_o)
    )
    grad_low, feed, held_wgu, grad_attn = tie(grad_low, feed, held_wgu, grad_attn)
    out_shard = (hidden + feed.astype(f32)).astype(bf16)
    grad_low, out_shard = tie(grad_low, out_shard)
    output = from_shards(out_shard)
    grad_later = exchange(grad_state, grad_low, False, own_end, near_end)
    grad_k, grad_v, grad_logits = run_finish(
        qkv, levels, one, sig, aux, sums, state_in, state_own, gk, gv, row_sums, acts, grad_later
    )
    decay_rows = lanes(grad_logits, (count, members))
    grad_all = jnp.concatenate(
        [a.reshape(rows, heads) for a in (grad_q, grad_k, grad_v)] + [decay_rows.T], axis=1
    )
    part_n1 = (matmul(grad_all[:, :cut], w_qkv, 1, 1) + matmul(decay_rows, w_dec, 0, 1)).astype(bf16)
    part_n1, output, grad_all = tie(part_n1, output, grad_all)
    grad_n1 = to_shards(part_n1)
    gain_one_part = jnp.sum(part_n1.astype(f32) * unit_one, axis=0)
    bias_part = lax.dynamic_update_slice_in_dim(
        jnp.zeros_like(decay_bias),
        jnp.sum(grad_logits.astype(f32), axis=1),
        tp_place * SLOTS,
        0,
    )
    small = jnp.concatenate(
        [gain_one_part, gain_two_part, jnp.sum(head_part, axis=(0, 1)), bias_part]
    )
    held_wo = scatter_first(scatter_cores(matmul(grad_attn, normed_heads, 0, 0).astype(bf16)))
    grad_in = matmul(normed1, grad_all, 0, 0).astype(bf16)
    held_in = scatter_cores(grad_in)
    grad_n1, small, held_in, held_wd = tie(grad_n1, small, held_in, held_wd)
    held_wgu, held_wo = scatter_second(held_wgu), scatter_second(held_wo)
    input_grad = grad_hidden + norm_back(mine(unit_one), mine(factor_one), grad_n1.astype(f32) * norm1_gain)
    input_grad = from_shards(input_grad)
    held_wd = scatter_second(held_wd)
    if places != 4:
        small = lax.psum(small, ("dp", "ctx", "tp"))
    else:
        small += lax.ppermute(small, "dp", [(0, 1), (1, 0)])
        for axis in ("ctx", "tp"):
            for r in (1, 2):
                small += lax.ppermute(small, axis, [(i, i ^ r) for i in range(4)])
    held_in = scatter_first(held_in)
    rows_wo, rows_wgu, rows_wd = scatter_end(held_wo), scatter_end(held_wgu), scatter_end(held_wd)
    rows_att = scatter_end(scatter_second(held_in))
    blocks_wo = [rows_wo[:, r * heads : (r + 1) * heads] for r in range(members)]
    distance = 1
    while len(blocks_wo) > 1:
        there = from_partner(jnp.concatenate(blocks_wo[1::2], axis=1).astype(bf16), distance)
        if 2 * distance == members:
            there, small = tie(there, small)
        blocks_wo = [
            block + there[:, i * heads : (i + 1) * heads].astype(f32)
            for i, block in enumerate(blocks_wo[::2])
        ]
        distance *= 2
    rows_wo = blocks_wo[0]
    input_grad = natural(input_grad).astype(f32)
    return (
        natural(output).reshape(count, tokens, width),
        input_grad.reshape(count, tokens, width),
        small[:width],
        small[width : 2 * width],
        small[2 * width : 2 * width + HEAD_DIM],
        small[2 * width + HEAD_DIM :],
        rows_att[:, :heads],
        rows_att[:, heads : 2 * heads],
        rows_att[:, 2 * heads : cut],
        rows_att[:, cut:],
        rows_wo.T,
        rows_wgu[:, :hidden_units],
        rows_wgu[:, hidden_units:],
        rows_wd.T,
    )


def solution(mesh):
    return jax.shard_map(
        per_device,
        mesh=mesh,
        in_specs=(
            P("dp", "ctx", None),
            P("dp", "ctx"),
            P("dp", "ctx", None),
            P(),
            P(),
            P(),
            P(),
            P(("dp", "ctx"), "tp"),
            P(("dp", "ctx"), "tp"),
            P(("dp", "ctx"), "tp"),
            P(("dp", "ctx"), "tp"),
            P("tp", ("dp", "ctx")),
            P(("dp", "ctx"), "tp"),
            P(("dp", "ctx"), "tp"),
            P("tp", ("dp", "ctx")),
        ),
        out_specs=(
            P("dp", "ctx", None),
            P("dp", "ctx", None),
            P(),
            P(),
            P(),
            P(),
            P(("dp", "ctx"), "tp"),
            P(("dp", "ctx"), "tp"),
            P(("dp", "ctx"), "tp"),
            P(("dp", "ctx"), "tp"),
            P("tp", ("dp", "ctx")),
            P(("dp", "ctx"), "tp"),
            P(("dp", "ctx"), "tp"),
            P("tp", ("dp", "ctx")),
        ),
        check_vma=False,
    )
```
